512 devices in a mesh: dp: 4 (over z_lo), tensor: 4 (over x), context: 32 (over z_hi, y, core).
Axes of the slice: x: 4, y: 8, z: 8 (z_hi: 2, z_lo: 4; z = z_hi * 4 + z_lo), core: 2. Of those that a mesh axis runs over, the one named last changes fastest.
Arguments:
- inputs: bfloat16 [4, 4096, 4096], P('dp', 'tensor', 'context'), may hold values from -6 to 6
- out_grad: bfloat16 [4, 4096, 4096], P('dp', 'tensor', 'context'), may hold values from -6 to 6
- filters: float32 [256, 4096], P('tensor', 'context'), may hold values from -0.09375 to 0.09375
- skip: float32 [4096], P('tensor'), may hold values from 0.5 to 1.5
Outputs:
- grad_input: bfloat16 [4, 4096, 4096], P('dp', 'tensor', 'context')
- grad_filter: float32 [256, 4096], P('tensor', 'context')
The draws below stay inside these ranges and needn't reach their ends.
All inputs are finite; a program needn't handle non-finite values.
Results may differ from the reference program's by a relative error of at most 0.0034.
Values may be sent and summed in bfloat16 or wider, within the bound.
A program may use at most 64 MiB of HBM per device.

```python
import math
import jax
import jax.numpy as jnp

GROUP = 16
GROUPS = 256
CHANNELS = 4096
SEQ = 4096
BATCH = 4


def levels(own_key, dims, shards, low, high):
    def one(position, parts):
        heights = jax.random.uniform(jax.random.fold_in(jax.random.fold_in(own_key, 6), position), (parts,), jnp.float32, low / len(shards), high / len(shards))
        return jnp.repeat(jnp.exp(heights), dims[position] // parts).reshape((-1,) + (1,) * (len(dims) - position - 1))

    level = one(*shards[0])
    for cut in shards[1:]:
        level = level * one(*cut)
    return level


def bell_draw(stream_key, extent, spread, most, shards=(), dtype=jnp.bfloat16):
    factor_of = levels(stream_key, extent, shards, -0.22, 0.18) if shards else 1.0
    drawn = jax.random.normal(stream_key, extent, jnp.float32) * spread * factor_of
    return jnp.minimum(jnp.maximum(drawn, -most), most).astype(dtype)


def setup_inputs(seed: int = 0) -> dict:
    arg_keys = jax.random.split(jax.random.key(seed), 5)
    inputs = bell_draw(arg_keys[0], (BATCH, CHANNELS, SEQ), 1.0, 6.0, ((0, 4), (1, 4), (2, 32)))
    out_grad = bell_draw(arg_keys[1], (BATCH, CHANNELS, SEQ), 1.0, 6.0, ((0, 4), (1, 4), (2, 32)))
    filters = bell_draw(arg_keys[2], (GROUPS, SEQ), SEQ ** -0.5, 0.09375, ((0, 4), (1, 32)), jnp.float32)
    skip = jnp.clip(0.5 + 1.0 * jax.random.uniform(arg_keys[3], (CHANNELS,), jnp.float32) ** levels(arg_keys[3], (CHANNELS,), ((0, 4),), -0.2, 0.2), 0.5, 1.5)
    return dict(inputs=inputs, out_grad=out_grad, filters=filters, skip=skip)


def reference(inputs, out_grad, filters, skip):
    padded_len = 2 * SEQ
    filter_spec = jnp.fft.rfft(filters, n=padded_len, axis=-1)
    channel_spec = jnp.repeat(filter_spec, GROUP, axis=0)
    gradients = []
    filter_sum = jnp.zeros((GROUPS, SEQ), jnp.float32)
    for sequence in range(BATCH):
        signal = inputs[sequence].astype(jnp.float32)
        upstream = out_grad[sequence].astype(jnp.float32)
        sig_spec = jnp.fft.rfft(signal, n=padded_len, axis=-1)
        up_spec = jnp.fft.rfft(upstream, n=padded_len, axis=-1)
        correlated = jnp.fft.irfft(jnp.conj(channel_spec) * up_spec, n=padded_len, axis=-1)[:, :SEQ]
        correlated = correlated.astype(jnp.float32).astype(jnp.bfloat16)
        gradients.append((correlated.astype(jnp.float32) + skip[:, None] * upstream).astype(jnp.bfloat16))
        lagged = jnp.fft.irfft(jnp.conj(sig_spec) * up_spec, n=padded_len, axis=-1)[:, :SEQ]
        filter_sum = filter_sum + lagged.reshape(GROUPS, GROUP, SEQ).sum(axis=1).astype(jnp.float32)
    norm_scale = 1.0 / math.sqrt(BATCH * GROUP * SEQ)
    return (jnp.stack(gradients), filter_sum * norm_scale)
```

```python
import functools
import math

import jax
import jax.numpy as jnp
from jax import lax
from jax.experimental import pallas as pl
from jax.experimental.pallas import tpu as pltpu
from jax.sharding import PartitionSpec as P

GROUP = 16
LANES = 128
MESH = pl.DeviceIdType.MESH
F32 = jnp.float32
BF16 = jnp.bfloat16


def whole_wait(ref, sem):
    pltpu.make_async_copy(ref, ref, sem).wait()


def shift_table(taps, pad):
    width = taps.shape[1] + pad
    rows = jnp.concatenate([taps, jnp.zeros((16, pad), F32)], axis=1)
    row = lax.broadcasted_iota(jnp.int32, (16, width), 0)
    for bit in (1, 2, 4, 8):
        rows = jnp.where(row % (2 * bit) >= bit, pltpu.roll(rows, bit, 1), rows)
    return rows


def kernel(sizes, x_in, g_in, f_in, s_in, gi_out, gf_out,
           f_send, f_all, g_all, x_all, toe_hi, toe_lo, acc, back, back_all,
           direct, lag_rows, lag_send, lag_all, g_here,
           s_send, s_recv, s_loc):
    owners, seqs, own_grp, scale = sizes
    blocks = owners // 2
    taps = owners * LANES
    me = lax.axis_index("context")
    seq = lax.axis_index("dp")
    core, place = me % 2, me // 2
    half = owners // 2

    def peer(k):
        v = (k + half) % owners + k // half
        far = (me // half + v // half) % 2
        near = (me % half // 2 + v % half // 2) % (half // 2)
        return far * half + near * 2 + (core + v) % 2

    def to_peers(body):
        def step(k, carry):
            body(peer(k))
            return carry

        lax.fori_loop(0, owners - 1, step, 0)

    barrier = pltpu.get_barrier_semaphore()
    to_peers(lambda o: pl.semaphore_signal(
        barrier, inc=1, device_id={"context": o}, device_id_type=MESH))
    for r in range(1, seqs):
        pl.semaphore_signal(
            barrier, inc=1, device_id={"dp": (seq + r) % seqs}, device_id_type=MESH)

    here = pltpu.make_async_copy(g_in, g_here, s_loc.at[0])
    here.start()
    for o in range(owners):
        f_send[o] = f_in[own_grp * o : own_grp * (o + 1), :]
    f_all[pl.ds(me, 1)] = f_send[pl.ds(me, 1)]
    g_all[:, :, blocks:] = jnp.zeros((2, own_grp, blocks, GROUP, LANES), BF16)

    mine = pl.ds(own_grp * me, own_grp)
    pltpu.make_async_copy(g_in.at[mine], g_all.at[core, :, place], s_recv.at[1]).start()
    pltpu.make_async_copy(x_in.at[mine], x_all.at[core, :, place], s_recv.at[2]).start()

    pl.semaphore_wait(barrier, owners - 1 + seqs - 1)

    def send(src, dst, k, where):
        pltpu.make_async_remote_copy(
            src_ref=src, dst_ref=dst, send_sem=s_send.at[k], recv_sem=s_recv.at[k],
            device_id=where, device_id_type=MESH).start()

    to_peers(lambda o: send(f_send.at[o], f_all.at[me], 0, {"context": o}))
    to_peers(lambda o: send(
        g_in.at[pl.ds(own_grp * o, own_grp)], g_all.at[core, :, place], 1, {"context": o}))
    to_peers(lambda o: send(
        x_in.at[pl.ds(own_grp * o, own_grp)], x_all.at[core, :, place], 2, {"context": o}))

    here.wait()
    by_row = s_in[...].T
    per = LANES // GROUP
    for m in range(s_in.shape[0]):
        part = g_here[per * m : per * (m + 1)].reshape(LANES, LANES).astype(F32)
        part = part * jnp.broadcast_to(by_row[:, m : m + 1], (LANES, LANES))
        direct[per * m : per * (m + 1)] = part.reshape(per, GROUP, LANES)

    whole_wait(f_all.at[pl.ds(0, owners - 1)], s_recv.at[0])
    for g in range(own_grp):
        lead = jnp.zeros((LANES, LANES), BF16)
        toe_hi[g, :, 0:LANES] = lead
        toe_lo[g, :, 0:LANES] = lead
        wide = jnp.concatenate(
            [jnp.broadcast_to(f_all[j, g : g + 1, :], (16, LANES)) for j in range(owners)],
            axis=1)
        rows = shift_table(wide, LANES)
        for q in range(LANES // 16):
            moved = rows if q == 0 else pltpu.roll(rows, 16 * q, 1)
            moved = moved[:, :taps]
            high = moved.astype(BF16)
            toe_hi[g, 16 * q : 16 * (q + 1), LANES:] = high
            toe_lo[g, 16 * q : 16 * (q + 1), LANES:] = (moved - high.astype(F32)).astype(BF16)

    def rows_of(ref, g, start, count):
        return jnp.concatenate(
            [ref[c, g, start : start + count].reshape(count * GROUP, LANES) for c in range(2)],
            axis=1)

    whole_wait(x_all, s_recv.at[1])
    step = min(4, blocks)
    for g in range(own_grp):
        for e in range(0, blocks, step):
            count = blocks - e
            left = jnp.concatenate(
                [rows_of(g_all, g, e + t, count) for t in range(step)], axis=1)
            lo, hi = 2 * LANES * e, 2 * LANES * (e + step)
            total = None
            for toe in (toe_lo, toe_hi):
                right = jnp.concatenate(
                    [toe[g, :, LANES + lo : LANES + hi], toe[g, :, lo:hi]], axis=0)
                term = lax.dot_general(
                    left, right, (((1,), (1,)), ((), ())), preferred_element_type=F32)
                total = term if total is None else total + term
            if e == 0:
                acc[...] = total
            else:
                acc[0 : count * GROUP] += total
        for c in range(2):
            back[c, g] = acc[:, LANES * c : LANES * (c + 1)].astype(BF16).reshape(
                blocks, GROUP, LANES)
        pltpu.make_async_copy(
            back.at[core, g, place], back_all.at[own_grp * me + g], s_recv.at[3]).start()
        to_peers(lambda o: send(
            back.at[o % 2, g, o // 2], back_all.at[own_grp * me + g], 3, {"context": o}))

    whole_wait(x_all, s_recv.at[2])
    for g in range(own_grp):
        turned = jnp.concatenate(
            [x_all[c, g].reshape(blocks * GROUP, LANES).T for c in range(2)], axis=0)
        carry = jnp.zeros((LANES, LANES), F32)
        for d in reversed(range(blocks)):
            square = jnp.dot(
                turned, rows_of(g_all, g, d, blocks), preferred_element_type=F32)
            at = 2 * LANES * d
            lag_rows[:, at : at + LANES] = square[:LANES, :LANES] + square[LANES:, LANES:]
            lag_rows[:, at + LANES : at + 2 * LANES] = square[:LANES, LANES:] + carry
            carry = square[LANES:, :LANES]
        width = taps + LANES
        total = None
        for q in reversed(range(LANES // 8)):
            row = jnp.concatenate(
                [jnp.zeros((8, LANES), F32), lag_rows[8 * q : 8 * (q + 1), :]], axis=1)
            total = row if total is None else row + pltpu.roll(total, width - 8, 1)
        row = lax.broadcasted_iota(jnp.int32, (8, width), 0)
        for bit in (1, 2, 4):
            total = jnp.where(
                row % (2 * bit) >= bit, pltpu.roll(total, width - bit, 1), total)
        line = jnp.sum(total, axis=0, keepdims=True)[:, LANES:]
        for j in range(owners):
            lag_send[j, g : g + 1, :] = line[:, LANES * j : LANES * (j + 1)]

    pltpu.make_async_copy(lag_send.at[me], lag_all.at[seq, me], s_recv.at[4]).start()
    to_peers(lambda o: send(lag_send.at[o], lag_all.at[seq, me], 4, {"context": o}))
    whole_wait(lag_all.at[0], s_recv.at[4])
    for r in range(1, seqs):
        send(lag_all.at[seq], lag_all.at[seq], 5, {"dp": (seq + r) % seqs})

    whole_wait(back_all, s_recv.at[3])
    gi_out[...] = (back_all[...].astype(F32) + direct[...]).astype(BF16)

    whole_wait(lag_all.at[pl.ds(0, seqs - 1)], s_recv.at[5])
    summed = lag_all[0]
    for b in range(1, seqs):
        summed = summed + lag_all[b]
    summed = summed * scale
    for o in range(owners):
        gf_out[own_grp * o : own_grp * (o + 1), :] = summed[o]

    others = own_grp * (owners - 1)
    whole_wait(f_send.at[pl.ds(0, owners - 1)], s_send.at[0])
    whole_wait(g_in.at[pl.ds(0, others)], s_send.at[1])
    whole_wait(x_in.at[pl.ds(0, others)], s_send.at[2])
    whole_wait(back_all.at[pl.ds(0, others)], s_send.at[3])
    whole_wait(lag_send.at[pl.ds(0, owners - 1)], s_send.at[4])
    whole_wait(lag_all.at[pl.ds(0, seqs - 1)], s_send.at[5])


def per_device(inputs, out_grad, filters, skip):
    channels, tok = inputs.shape[1], inputs.shape[2]
    groups = filters.shape[0]
    owners, seqs = lax.axis_size("context"), lax.axis_size("dp")
    own_grp = groups // owners
    blocks = owners // 2
    scale = 1.0 / math.sqrt(seqs * GROUP * tok * owners)
    vmem = pl.BlockSpec(memory_space=pltpu.VMEM)
    anywhere = pl.BlockSpec(memory_space=pl.ANY)
    tiles = (groups, GROUP, LANES)
    held = (2, own_grp, blocks, GROUP, LANES)
    grad_input, grad_filter = pl.pallas_call(
        functools.partial(kernel, (owners, seqs, own_grp, scale)),
        out_shape=(
            jax.ShapeDtypeStruct(tiles, BF16),
            jax.ShapeDtypeStruct((groups, LANES), F32),
        ),
        in_specs=[anywhere, anywhere, vmem, vmem],
        out_specs=(vmem, vmem),
        scratch_shapes=[
            pltpu.VMEM((owners, own_grp, LANES), F32),
            pltpu.VMEM((owners, own_grp, LANES), F32),
            pltpu.VMEM((2, own_grp, 2 * blocks, GROUP, LANES), BF16),
            pltpu.VMEM(held, BF16),
            pltpu.VMEM((own_grp, LANES, LANES * (owners + 1)), BF16),
            pltpu.VMEM((own_grp, LANES, LANES * (owners + 1)), BF16),
            pltpu.VMEM((blocks * GROUP, 2 * LANES), F32),
            pltpu.VMEM(held, BF16),
            pltpu.VMEM(tiles, BF16),
            pltpu.VMEM(tiles, F32),
            pltpu.VMEM((LANES, LANES * owners), F32),
            pltpu.VMEM((owners, own_grp, LANES), F32),
            pltpu.VMEM((seqs, owners, own_grp, LANES), F32),
            pltpu.VMEM(tiles, BF16),
            pltpu.SemaphoreType.DMA((6,)),
            pltpu.SemaphoreType.DMA((6,)),
            pltpu.SemaphoreType.DMA((1,)),
        ],
        compiler_params=pltpu.CompilerParams(
            collective_id=0, has_side_effects=True, vmem_limit_bytes=48 * 1024 * 1024),
    )(
        inputs.reshape(tiles),
        out_grad.reshape(tiles),
        filters,
        skip.reshape(channels // LANES, LANES),
    )
    return grad_input.reshape(1, channels, tok), grad_filter


def solution(mesh):
    placed = (
        P("dp", "tensor", "context"),
        P("dp", "tensor", "context"),
        P("tensor", "context"),
        P("tensor"),
    )
    return jax.shard_map(
        per_device,
        mesh=mesh,
        in_specs=placed,
        out_specs=(P("dp", "tensor", "context"), P("tensor", "context")),
        check_vma=False,
    )
```

```python
import functools
import math

import jax
import jax.numpy as jnp
from jax import lax
from jax.experimental import pallas as pl
from jax.experimental.pallas import tpu as pltpu
from jax.sharding import PartitionSpec as P

GROUP = 16
LANES = 128
PAIR = 256
MESH = pl.DeviceIdType.MESH
F32 = jnp.float32
BF16 = jnp.bfloat16

TAPS_LOW, TAPS_HIGH, NEAR_GRAD, NEAR_IN, FAR_GRAD, BACK, TERMS_LOW, TERMS_HIGH, FINAL, TAPS_CROSS = (
    0, 1, 2, 3, 4, 6, 7, 8, 9, 10)
N_SEMS = 11


def whole_wait(ref, sem):
    pltpu.make_async_copy(ref, ref, sem).wait()


def kernel(sizes, x_hbm, g_hbm, f_hbm, s_hbm, gi_out, gf_out,
           f_here, s_here, g_here, f_send, f_all, near, far, x_all, turned, toe, acc, back,
           back_all, direct, lag_rows, lag_send, lag_in, lag_fin, gf_all,
           s_send, s_recv, s_loc, ready):
    owners, seqs, scale = sizes
    half = owners // 2
    own = f_send.shape[1]
    own_groups = own
    blocks = half // 2
    low_taps = half * LANES
    part = owners // seqs
    chunk = own // 2
    me = lax.axis_index("context")
    seq = lax.axis_index("dp")
    z, h = me // half, me % half
    core, place = h % 2, h // 2
    is_low, is_high = z == 0, z == 1

    def send(src, dst, k, where):
        pltpu.make_async_remote_copy(
            src_ref=src, dst_ref=dst, send_sem=s_send.at[k], recv_sem=s_recv.at[k],
            device_id=where, device_id_type=MESH).start()

    def local(src, dst, k):
        pltpu.make_async_copy(src, dst, s_recv.at[k]).start()

    def loop(first, body):
        def step(k, carry):
            body((h + k) % half)
            return carry

        lax.fori_loop(first, half, step, 0)

    def signal(where):
        pl.semaphore_signal(barrier, inc=1, device_id=where, device_id_type=MESH)

    barrier = pltpu.get_barrier_semaphore()
    loop(1, lambda o: signal({"context": z * half + o}))

    @pl.when(is_low)
    def _():
        loop(0, lambda o: signal({"context": half + o}))
        for r in range(1, seqs):
            signal({"dp": (seq + r) % seqs})
            signal({"dp": (seq + r) % seqs, "context": half + h})

    stage = [
        pltpu.make_async_copy(f_hbm, f_here, s_loc.at[0]),
        pltpu.make_async_copy(s_hbm, s_here, s_loc.at[1]),
        pltpu.make_async_copy(g_hbm, g_here, s_loc.at[2]),
    ]
    for copy in stage:
        copy.start()
    mine = pl.ds(own * h, own)
    local(g_hbm.at[mine], near.at[core, :, place], NEAR_GRAD)
    local(x_hbm.at[mine], x_all.at[core, :, place], NEAR_IN)
    zeros = jnp.zeros((2, own, blocks, GROUP, LANES), BF16)

    stage[0].wait()
    for o in range(half):
        f_send[o] = f_here[own * o : own * (o + 1), :]

    @pl.when(is_high)
    def _():
        pl.semaphore_wait(barrier, half - 1 + half + seqs - 1)
        pl.semaphore_signal(ready, inc=1, device_id={"context": h}, device_id_type=MESH)
        loop(0, lambda o: send(f_send.at[o], f_all.at[me], TAPS_HIGH, {"context": o}))
        for c in range(2):
            loop(0, lambda o: send(
                g_hbm.at[pl.ds(own * o + chunk * c, chunk)],
                far.at[core, pl.ds(chunk * c, chunk), blocks + place],
                FAR_GRAD + c, {"context": o}))

    @pl.when(is_low)
    def _():
        pl.semaphore_wait(barrier, half - 1 + seqs - 1)
        loop(1, lambda o: send(f_send.at[o], f_all.at[me], TAPS_LOW, {"context": o}))
        local(f_send.at[h], f_all.at[me], TAPS_LOW)

    loop(1, lambda o: send(
        g_hbm.at[pl.ds(own * o, own)], near.at[core, :, place], NEAR_GRAD,
        {"context": z * half + o}))
    loop(1, lambda o: send(
        x_hbm.at[pl.ds(own * o, own)], x_all.at[core, :, place], NEAR_IN,
        {"context": z * half + o}))

    near[:, :, blocks:] = zeros

    stage[1].wait()
    stage[2].wait()
    by_row = s_here[...].T
    per = LANES // GROUP
    for m in range(s_here.shape[0]):
        piece = g_here[per * m : per * (m + 1)].reshape(LANES, LANES).astype(F32)
        piece = piece * jnp.broadcast_to(by_row[:, m : m + 1], (LANES, LANES))
        direct[per * m : per * (m + 1)] = piece.reshape(per, GROUP, LANES)

    def build(g, first):
        lead = (
            jnp.zeros((GROUP, LANES), F32) if first == 0
            else jnp.broadcast_to(f_all[first - 1, g : g + 1, :], (GROUP, LANES)))
        rows = jnp.concatenate(
            [lead] + [
                jnp.broadcast_to(f_all[j, g : g + 1, :], (GROUP, LANES))
                for j in range(first, first + half)],
            axis=1)
        row = lax.broadcasted_iota(jnp.int32, rows.shape, 0)
        for bit in (1, 2, 4, 8):
            rows = jnp.where(row % (2 * bit) >= bit, pltpu.roll(rows, bit, 1), rows)
        at = LANES * (first + 1)
        if first == 0:
            toe[g, :, 0:LANES] = jnp.zeros((LANES, LANES), BF16)
        for q in range(LANES // GROUP):
            moved = rows if q == 0 else pltpu.roll(rows, GROUP * q, 1)
            toe[g, GROUP * q : GROUP * (q + 1), at : at + low_taps] = (
                moved[:, LANES:].astype(BF16))

    def rows_of(ref, g, start, count):
        return jnp.concatenate(
            [ref[c, g, start : start + count].reshape(count * GROUP, LANES) for c in range(2)],
            axis=1)

    def against_toe(ref, g, first, last, count):
        left = jnp.concatenate([rows_of(ref, g, d, count) for d in range(first, last)], axis=1)
        lo, hi = PAIR * first, PAIR * last
        right = jnp.concatenate(
            [toe[g, :, LANES + lo : LANES + hi], toe[g, :, lo:hi]], axis=0)
        return lax.dot_general(
            left, right, (((1,), (1,)), ((), ())), preferred_element_type=F32)

    def near_correlation(g):
        step = min(4, blocks)
        for e in range(0, blocks, step):
            count = blocks - e
            term = against_toe(near, g, e, e + step, count)
            if e == 0:
                acc[g] = term
            else:
                acc[g, 0 : count * GROUP] += term

    def far_correlation(g):
        total = acc[g]
        for e in range(0, 2 * blocks, 4):
            total = total + against_toe(far, g, e, e + 4, blocks)
        acc[g] = total

    def send_back(first, count):
        for g in range(first, first + count):
            for c in range(2):
                back[c, g] = acc[g, :, LANES * c : LANES * (c + 1)].astype(BF16).reshape(
                    blocks, GROUP, LANES)
        which = pl.ds(first, count)
        where = pl.ds(own * h + first, count)
        local(back.at[core, which, place], back_all.at[where], BACK)
        loop(1, lambda o: send(
            back.at[o % 2, which, o // 2], back_all.at[where], BACK,
            {"context": z * half + o}))

    def near_lags(g):
        left = jnp.concatenate(
            [x_all[c, g].reshape(blocks * GROUP, LANES).T for c in range(2)], axis=0)
        turned[g] = left
        carry = jnp.zeros((LANES, LANES), F32)
        for d in reversed(range(blocks)):
            square = jnp.dot(left, rows_of(near, g, d, blocks), preferred_element_type=F32)
            at = PAIR * d
            lag_rows[g, :, at : at + LANES] = square[:LANES, :LANES] + square[LANES:, LANES:]
            lag_rows[g, :, at + LANES : at + PAIR] = square[:LANES, LANES:] + carry
            carry = square[LANES:, :LANES]

    def far_lags(g):
        left = turned[g]
        carry = jnp.zeros((LANES, LANES), F32)
        for d in reversed(range(1, 2 * blocks)):
            square = jnp.dot(left, rows_of(far, g, d, blocks), preferred_element_type=F32)
            at = PAIR * d
            even = square[:LANES, :LANES] + square[LANES:, LANES:]
            odd = square[:LANES, LANES:] + carry
            if d < blocks:
                even = even + lag_rows[g, :, at : at + LANES]
                odd = odd + lag_rows[g, :, at + LANES : at + PAIR]
            lag_rows[g, :, at : at + LANES] = even
            lag_rows[g, :, at + LANES : at + PAIR] = odd
            carry = square[LANES:, :LANES]
        lag_rows[g, :, LANES:PAIR] += carry

    def diagonals(g, taps):
        width = taps + LANES
        rows = [
            jnp.concatenate(
                [jnp.zeros((8, LANES), F32), lag_rows[g, 8 * q : 8 * (q + 1), :taps]], axis=1)
            for q in range(LANES // 8)]
        move = 8
        while len(rows) > 1:
            rows = [
                rows[k] + pltpu.roll(rows[k + 1], width - move, 1)
                for k in range(0, len(rows), 2)]
            move = 2 * move
        total = rows[0]
        row = lax.broadcasted_iota(jnp.int32, (8, width), 0)
        for bit in (1, 2, 4):
            total = jnp.where(
                row % (2 * bit) >= bit, pltpu.roll(total, width - bit, 1), total)
        line = jnp.sum(total, axis=0, keepdims=True)[:, LANES:]
        for j in range(taps // LANES):
            lag_send[j, g : g + 1, :] = line[:, LANES * j : LANES * (j + 1)]

    @pl.when(is_high)
    def _():
        whole_wait(f_all.at[pl.ds(0, half)], s_recv.at[TAPS_CROSS])
        for g in range(own_groups):
            build(g, 0)
        whole_wait(x_all, s_recv.at[NEAR_GRAD])
        for g in range(own_groups):
            near_correlation(g)
        send_back(0, own)
        whole_wait(x_all, s_recv.at[NEAR_IN])
        for g in range(own_groups):
            near_lags(g)
            diagonals(g, low_taps)
        for p in range(seqs // 2):
            send(lag_send.at[pl.ds(part * p, part)], lag_in.at[1, seq], TERMS_HIGH,
                 {"dp": p, "context": h})
        whole_wait(back_all, s_recv.at[BACK])

    @pl.when(is_low)
    def _():
        far[:, :, 0:blocks] = zeros
        far[:, :, 2 * blocks :] = zeros
        whole_wait(f_all.at[pl.ds(0, half)], s_recv.at[TAPS_LOW])
        for g in range(own_groups):
            build(g, 0)
        pl.semaphore_wait(ready, 1)
        low = f_all.at[pl.ds(0, half)]
        send(low, low, TAPS_CROSS, {"context": half + h})
        whole_wait(x_all, s_recv.at[NEAR_GRAD])
        for g in range(own_groups):
            near_correlation(g)
        whole_wait(x_all, s_recv.at[NEAR_IN])
        for g in range(own_groups):
            near_lags(g)

        whole_wait(f_all.at[pl.ds(half, half)], s_recv.at[TAPS_HIGH])
        for g in range(own_groups):
            build(g, half)
        first = far.at[:, pl.ds(0, chunk), pl.ds(blocks, blocks)]
        whole_wait(first, s_recv.at[FAR_GRAD])
        for g in range(chunk):
            far_correlation(g)
        send_back(0, chunk)
        for g in range(chunk):
            far_lags(g)
            diagonals(g, 2 * low_taps)
        whole_wait(first, s_recv.at[FAR_GRAD + 1])
        for g in range(chunk, own):
            far_lags(g)
            diagonals(g, 2 * low_taps)
        local(lag_send.at[pl.ds(part * seq, part)], lag_in.at[0, seq], TERMS_LOW)
        for r in range(1, seqs):
            p = (seq + r) % seqs
            send(lag_send.at[pl.ds(part * p, part)], lag_in.at[0, seq], TERMS_LOW, {"dp": p})
        for g in range(chunk, own):
            far_correlation(g)
        send_back(chunk, own - chunk)

        whole_wait(lag_in.at[0], s_recv.at[TERMS_LOW])
        summed = lag_in[0, 0]
        for b in range(1, seqs):
            summed = summed + lag_in[0, b]
        lag_fin[...] = summed * scale

        @pl.when(seq < seqs // 2)
        def _():
            whole_wait(lag_in.at[1], s_recv.at[TERMS_HIGH])
            more = lag_in[1, 0]
            for b in range(1, seqs):
                more = more + lag_in[1, b]
            lag_fin[...] += more * scale

        def deliver(k, carry):
            at = seq * part + k % part
            to = (seq + k // part) % seqs

            @pl.when((at != me) | (to != seq))
            def _():
                send(lag_fin.at[k % part], gf_all.at[h], FINAL, {"dp": to, "context": at})

            return carry

        lax.fori_loop(0, owners, deliver, 0)

        @pl.when(me // part == seq)
        def _():
            local(lag_fin.at[me % part], gf_all.at[h], FINAL)

        whole_wait(back_all, s_recv.at[BACK])

    gi_out[...] = (back_all[...].astype(F32) + direct[...]).astype(BF16)
    whole_wait(gf_all, s_recv.at[FINAL])
    for o in range(half):
        gf_out[own * o : own * (o + 1), :] = gf_all[o]

    others = own * (half - 1)
    whole_wait(g_hbm.at[pl.ds(0, others)], s_send.at[NEAR_GRAD])
    whole_wait(x_hbm.at[pl.ds(0, others)], s_send.at[NEAR_IN])
    whole_wait(back_all.at[pl.ds(0, others)], s_send.at[BACK])

    @pl.when(is_high)
    def _():
        whole_wait(f_send, s_send.at[TAPS_HIGH])
        for c in range(2):
            whole_wait(g_hbm.at[pl.ds(0, chunk * half)], s_send.at[FAR_GRAD + c])
        whole_wait(lag_send.at[pl.ds(0, part * (seqs // 2))], s_send.at[TERMS_HIGH])

    @pl.when(is_low)
    def _():
        whole_wait(f_all.at[pl.ds(0, half - 1)], s_send.at[TAPS_LOW])
        whole_wait(f_all.at[pl.ds(0, half)], s_send.at[TAPS_CROSS])
        whole_wait(lag_send.at[pl.ds(0, part * (seqs - 1))], s_send.at[TERMS_LOW])

        @pl.when(me // part == seq)
        def _():
            whole_wait(lag_send.at[pl.ds(0, owners - 1)], s_send.at[FINAL])

        @pl.when(me // part != seq)
        def _():
            whole_wait(lag_send, s_send.at[FINAL])


def per_device(inputs, out_grad, filters, skip):
    channels, tok = inputs.shape[1], inputs.shape[2]
    groups = filters.shape[0]
    owners, seqs = lax.axis_size("context"), lax.axis_size("dp")
    half = owners // 2
    own = groups // half
    blocks = half // 2
    part = owners // seqs
    scale = 1.0 / math.sqrt(seqs * GROUP * tok * owners)
    vmem = pl.BlockSpec(memory_space=pltpu.VMEM)
    hbm = pl.BlockSpec(memory_space=pltpu.HBM)
    tiles = (groups, GROUP, LANES)
    held = (2, own, blocks, GROUP, LANES)
    grad_input, grad_filter = pl.pallas_call(
        functools.partial(kernel, (owners, seqs, scale)),
        out_shape=(
            jax.ShapeDtypeStruct(tiles, BF16),
            jax.ShapeDtypeStruct((groups, LANES), F32),
        ),
        in_specs=[hbm, hbm, hbm, hbm],
        out_specs=(vmem, vmem),
        scratch_shapes=[
            pltpu.VMEM((groups, LANES), F32),
            pltpu.VMEM((channels // LANES, LANES), F32),
            pltpu.VMEM(tiles, BF16),
            pltpu.VMEM((half, own, LANES), F32),
            pltpu.VMEM((owners, own, LANES), F32),
            pltpu.VMEM((2, own, 2 * blocks, GROUP, LANES), BF16),
            pltpu.VMEM((2, own, 3 * blocks, GROUP, LANES), BF16),
            pltpu.VMEM(held, BF16),
            pltpu.VMEM((own, PAIR, blocks * GROUP), BF16),
            pltpu.VMEM((own, LANES, LANES * (owners + 1)), BF16),
            pltpu.VMEM((own, blocks * GROUP, PAIR), F32),
            pltpu.VMEM(held, BF16),
            pltpu.VMEM(tiles, BF16),
            pltpu.VMEM(tiles, F32),
            pltpu.VMEM((own, LANES, LANES * owners), F32),
            pltpu.VMEM((owners, own, LANES), F32),
            pltpu.VMEM((2, seqs, part, own, LANES), F32),
            pltpu.VMEM((part, own, LANES), F32),
            pltpu.VMEM((half, own, LANES), F32),
            pltpu.SemaphoreType.DMA((N_SEMS,)),
            pltpu.SemaphoreType.DMA((N_SEMS,)),
            pltpu.SemaphoreType.DMA((3,)),
            pltpu.SemaphoreType.REGULAR,
        ],
        compiler_params=pltpu.CompilerParams(
            collective_id=0, has_side_effects=True, vmem_limit_bytes=56 * 1024 * 1024),
    )(
        inputs.reshape(tiles),
        out_grad.reshape(tiles),
        filters,
        skip.reshape(channels // LANES, LANES),
    )
    return grad_input.reshape(1, channels, tok), grad_filter


def solution(mesh):
    placed = (
        P("dp", "tensor", "context"),
        P("dp", "tensor", "context"),
        P("tensor", "context"),
        P("tensor"),
    )
    return jax.shard_map(
        per_device,
        mesh=mesh,
        in_specs=placed,
        out_specs=(P("dp", "tensor", "context"), P("tensor", "context")),
        check_vma=False,
    )
```

```python
import functools
import math

import jax
import jax.numpy as jnp
from jax import lax
from jax.experimental import pallas as pl
from jax.experimental.pallas import tpu as pltpu
from jax.sharding import PartitionSpec as P

GROUP = 16
LANES = 128
PAIR = 256
MESH = pl.DeviceIdType.MESH
F32 = jnp.float32
BF16 = jnp.bfloat16

TAPS_LOW, TAPS_HIGH, TAPS_CROSS, NEAR_IN, BACK, TERMS_LOW, TERMS_HIGH, FINAL = range(8)
NEAR_GRAD, FAR_GRAD = 8, 10
N_SEMS = 12


def whole_wait(ref, sem):
    pltpu.make_async_copy(ref, ref, sem).wait()


def kernel(sizes, x_hbm, g_hbm, f_hbm, s_hbm, gi_out, gf_out,
           f_here, s_here, g_here, f_send, f_all, near, far, x_all, turned, toe, acc, back,
           back_all, direct, lag_rows, lag_send, lag_in, lag_fin, gf_all,
           s_send, s_recv, s_loc, ready):
    owners, seqs, scale = sizes
    half = owners // 2
    own = f_send.shape[1]
    blocks = half // 2
    low_taps = half * LANES
    part = owners // seqs
    me = lax.axis_index("context")
    seq = lax.axis_index("dp")
    z, h = me // half, me % half
    core, place = h % 2, h // 2
    is_low, is_high = z == 0, z == 1

    def send(src, dst, k, where):
        pltpu.make_async_remote_copy(
            src_ref=src, dst_ref=dst, send_sem=s_send.at[k], recv_sem=s_recv.at[k],
            device_id=where, device_id_type=MESH).start()

    def local(src, dst, k):
        pltpu.make_async_copy(src, dst, s_recv.at[k]).start()

    def loop(first, body):
        def step(k, carry):
            body((h + k) % half)
            return carry

        lax.fori_loop(first, half, step, 0)

    def signal(where):
        pl.semaphore_signal(barrier, inc=1, device_id=where, device_id_type=MESH)

    barrier = pltpu.get_barrier_semaphore()
    loop(1, lambda o: signal({"context": z * half + o}))

    @pl.when(is_low)
    def _():
        loop(0, lambda o: signal({"context": half + o}))
        for r in range(1, seqs):
            signal({"dp": (seq + r) % seqs})
            signal({"dp": (seq + r) % seqs, "context": half + h})

    stage = [
        pltpu.make_async_copy(f_hbm, f_here, s_loc.at[0]),
        pltpu.make_async_copy(s_hbm, s_here, s_loc.at[1]),
        pltpu.make_async_copy(g_hbm, g_here, s_loc.at[2]),
    ]
    for copy in stage:
        copy.start()
    mine = pl.ds(own * h, own)
    count = own // 2
    for k in range(2):
        local(g_hbm.at[pl.ds(own * h + count * k, count)],
              near.at[core, pl.ds(count * k, count), place], NEAR_GRAD + k)
    local(x_hbm.at[mine], x_all.at[core, :, place], NEAR_IN)
    zeros = jnp.zeros((2, own, blocks, GROUP, LANES), BF16)

    stage[0].wait()
    for o in range(half):
        f_send[o] = f_here[own * o : own * (o + 1), :]

    @pl.when(is_high)
    def _():
        pl.semaphore_wait(barrier, half - 1 + half + seqs - 1)
        pl.semaphore_signal(ready, inc=1, device_id={"context": h}, device_id_type=MESH)
        loop(0, lambda o: send(f_send.at[o], f_all.at[me], TAPS_HIGH, {"context": o}))
        loop(0, lambda o: send(
            g_hbm.at[pl.ds(own * o, count)], far.at[core, pl.ds(0, count), blocks + place],
            FAR_GRAD, {"context": o}))

    @pl.when(is_low)
    def _():
        pl.semaphore_wait(barrier, half - 1 + seqs - 1)
        loop(1, lambda o: send(f_send.at[o], f_all.at[me], TAPS_LOW, {"context": o}))
        local(f_send.at[h], f_all.at[me], TAPS_LOW)

    for k in (1, 0):
        loop(1, lambda o: send(
            g_hbm.at[pl.ds(own * o + count * k, count)],
            near.at[core, pl.ds(count * k, count), place], NEAR_GRAD + k,
            {"context": z * half + o}))
    loop(1, lambda o: send(
        x_hbm.at[pl.ds(own * o, own)], x_all.at[core, :, place], NEAR_IN,
        {"context": z * half + o}))

    near[:, :, blocks:] = zeros

    stage[1].wait()
    stage[2].wait()
    by_row = s_here[...].T
    per = LANES // GROUP
    for m in range(s_here.shape[0]):
        piece = g_here[per * m : per * (m + 1)].reshape(LANES, LANES).astype(F32)
        piece = piece * jnp.broadcast_to(by_row[:, m : m + 1], (LANES, LANES))
        direct[per * m : per * (m + 1)] = piece.reshape(per, GROUP, LANES)

    def build(g, first):
        lead = (
            jnp.zeros((GROUP, LANES), F32) if first == 0
            else jnp.broadcast_to(f_all[first - 1, g : g + 1, :], (GROUP, LANES)))
        rows = jnp.concatenate(
            [lead] + [
                jnp.broadcast_to(f_all[j, g : g + 1, :], (GROUP, LANES))
                for j in range(first, first + half)],
            axis=1)
        row = lax.broadcasted_iota(jnp.int32, rows.shape, 0)
        for bit in (1, 2, 4, 8):
            rows = jnp.where(row % (2 * bit) >= bit, pltpu.roll(rows, bit, 1), rows)
        at = LANES * (first + 1)
        if first == 0:
            toe[g, :, 0:LANES] = jnp.zeros((LANES, LANES), BF16)
        for q in range(LANES // GROUP):
            moved = rows if q == 0 else pltpu.roll(rows, GROUP * q, 1)
            toe[g, GROUP * q : GROUP * (q + 1), at : at + low_taps] = (
                moved[:, LANES:].astype(BF16))

    def rows_of(ref, g, start, count):
        return jnp.concatenate(
            [ref[c, g, start : start + count].reshape(count * GROUP, LANES) for c in range(2)],
            axis=1)

    def against_toe(ref, g, first, last, count):
        left = jnp.concatenate([rows_of(ref, g, d, count) for d in range(first, last)], axis=1)
        lo, hi = PAIR * first, PAIR * last
        right = jnp.concatenate(
            [toe[g, :, LANES + lo : LANES + hi], toe[g, :, lo:hi]], axis=0)
        return lax.dot_general(
            left, right, (((1,), (1,)), ((), ())), preferred_element_type=F32)

    def near_correlation(g):
        step = min(4, blocks)
        for e in range(0, blocks, step):
            count = blocks - e
            term = against_toe(near, g, e, e + step, count)
            if e == 0:
                acc[g] = term
            else:
                acc[g, 0 : count * GROUP] += term

    def far_correlation(g):
        total = acc[g]
        for e in range(0, 2 * blocks, 4):
            total = total + against_toe(far, g, e, e + 4, blocks)
        acc[g] = total

    def send_back(first, count):
        for g in range(first, first + count):
            for c in range(2):
                back[c, g] = acc[g, :, LANES * c : LANES * (c + 1)].astype(BF16).reshape(
                    blocks, GROUP, LANES)
        which = pl.ds(first, count)
        where = pl.ds(own * h + first, count)
        local(back.at[core, which, place], back_all.at[where], BACK)
        loop(1, lambda o: send(
            back.at[o % 2, which, o // 2], back_all.at[where], BACK,
            {"context": z * half + o}))

    def near_lags(g):
        left = jnp.concatenate(
            [x_all[c, g].reshape(blocks * GROUP, LANES).T for c in range(2)], axis=0)
        turned[g] = left
        carry = jnp.zeros((LANES, LANES), F32)
        for d in reversed(range(blocks)):
            square = jnp.dot(left, rows_of(near, g, d, blocks), preferred_element_type=F32)
            at = PAIR * d
            lag_rows[g, :, at : at + LANES] = square[:LANES, :LANES] + square[LANES:, LANES:]
            lag_rows[g, :, at + LANES : at + PAIR] = square[:LANES, LANES:] + carry
            carry = square[LANES:, :LANES]

    def far_lags(g):
        left = turned[g]
        carry = jnp.zeros((LANES, LANES), F32)
        for d in reversed(range(1, 2 * blocks)):
            square = jnp.dot(left, rows_of(far, g, d, blocks), preferred_element_type=F32)
            at = PAIR * d
            even = square[:LANES, :LANES] + square[LANES:, LANES:]
            odd = square[:LANES, LANES:] + carry
            if d < blocks:
                even = even + lag_rows[g, :, at : at + LANES]
                odd = odd + lag_rows[g, :, at + LANES : at + PAIR]
            lag_rows[g, :, at : at + LANES] = even
            lag_rows[g, :, at + LANES : at + PAIR] = odd
            carry = square[LANES:, :LANES]
        lag_rows[g, :, LANES:PAIR] += carry

    def diagonals(g, taps):
        width = taps + LANES
        rows = [
            jnp.concatenate(
                [jnp.zeros((8, LANES), F32), lag_rows[g, 8 * q : 8 * (q + 1), :taps]], axis=1)
            for q in range(LANES // 8)]
        move = 8
        while len(rows) > 1:
            rows = [
                rows[k] + pltpu.roll(rows[k + 1], width - move, 1)
                for k in range(0, len(rows), 2)]
            move = 2 * move
        total = rows[0]
        row = lax.broadcasted_iota(jnp.int32, (8, width), 0)
        for bit in (1, 2, 4):
            total = jnp.where(
                row % (2 * bit) >= bit, pltpu.roll(total, width - bit, 1), total)
        line = jnp.sum(total, axis=0, keepdims=True)[:, LANES:]
        for j in range(taps // LANES):
            lag_send[j, g : g + 1, :] = line[:, LANES * j : LANES * (j + 1)]

    def near_grad(k):
        return near.at[:, pl.ds(count * k, count), pl.ds(0, blocks)]

    def far_grad(k):
        return far.at[:, pl.ds(count * k, count), pl.ds(blocks, blocks)]

    @pl.when(is_high)
    def _():
        whole_wait(near_grad(1), s_recv.at[NEAR_GRAD + 1])
        send(near_grad(1), far_grad(1), FAR_GRAD + 1, {"context": h})
        whole_wait(f_all.at[pl.ds(0, half)], s_recv.at[TAPS_CROSS])
        for g in range(own):
            build(g, 0)
        whole_wait(near_grad(0), s_recv.at[NEAR_GRAD])
        for g in range(own):
            near_correlation(g)
        send_back(0, own)
        whole_wait(x_all, s_recv.at[NEAR_IN])
        for g in range(own):
            near_lags(g)
        for g in range(own):
            diagonals(g, low_taps)
        for p in range(seqs // 2):
            send(lag_send.at[pl.ds(part * p, part)], lag_in.at[1, seq], TERMS_HIGH,
                 {"dp": p, "context": h})
        whole_wait(back_all, s_recv.at[BACK])

    @pl.when(is_low)
    def _():
        far[:, :, 0:blocks] = zeros
        far[:, :, 2 * blocks :] = zeros
        whole_wait(f_all.at[pl.ds(0, half)], s_recv.at[TAPS_LOW])
        for g in range(own):
            build(g, 0)
        pl.semaphore_wait(ready, 1)
        low = f_all.at[pl.ds(0, half)]
        send(low, low, TAPS_CROSS, {"context": half + h})
        for k in (1, 0):
            whole_wait(near_grad(k), s_recv.at[NEAR_GRAD + k])
            for g in range(count * k, count * (k + 1)):
                near_correlation(g)
        whole_wait(f_all.at[pl.ds(half, half)], s_recv.at[TAPS_HIGH])
        for g in range(own):
            build(g, half)
        whole_wait(x_all, s_recv.at[NEAR_IN])
        for g in range(own):
            near_lags(g)
        pairs = (range(0, count), range(count, own))
        for k, some in enumerate(pairs):
            whole_wait(far_grad(k), s_recv.at[FAR_GRAD + k])
            for g in some:
                far_lags(g)
            for g in some:
                diagonals(g, 2 * low_taps)
        local(lag_send.at[pl.ds(part * seq, part)], lag_in.at[0, seq], TERMS_LOW)
        for r in range(1, seqs):
            p = (seq + r) % seqs
            send(lag_send.at[pl.ds(part * p, part)], lag_in.at[0, seq], TERMS_LOW, {"dp": p})
        for some in pairs:
            for g in some:
                far_correlation(g)
            send_back(some[0], len(some))

        whole_wait(lag_in.at[0], s_recv.at[TERMS_LOW])
        summed = lag_in[0, 0]
        for b in range(1, seqs):
            summed = summed + lag_in[0, b]
        lag_fin[...] = summed * scale

        @pl.when(seq < seqs // 2)
        def _():
            whole_wait(lag_in.at[1], s_recv.at[TERMS_HIGH])
            more = lag_in[1, 0]
            for b in range(1, seqs):
                more = more + lag_in[1, b]
            lag_fin[...] += more * scale

        def deliver(k, carry):
            at = seq * part + k % part
            to = (seq + k // part) % seqs

            @pl.when((at != me) | (to != seq))
            def _():
                send(lag_fin.at[k % part], gf_all.at[h], FINAL, {"dp": to, "context": at})

            return carry

        lax.fori_loop(0, owners, deliver, 0)

        @pl.when(me // part == seq)
        def _():
            local(lag_fin.at[me % part], gf_all.at[h], FINAL)

        whole_wait(back_all, s_recv.at[BACK])

    gi_out[...] = (back_all[...].astype(F32) + direct[...]).astype(BF16)
    whole_wait(gf_all, s_recv.at[FINAL])
    for o in range(half):
        gf_out[own * o : own * (o + 1), :] = gf_all[o]

    others = own * (half - 1)
    for k in range(2):
        whole_wait(g_hbm.at[pl.ds(0, count * (half - 1))], s_send.at[NEAR_GRAD + k])
    whole_wait(x_hbm.at[pl.ds(0, others)], s_send.at[NEAR_IN])
    whole_wait(back_all.at[pl.ds(0, others)], s_send.at[BACK])

    @pl.when(is_high)
    def _():
        whole_wait(f_send, s_send.at[TAPS_HIGH])
        for k in range(2):
            whole_wait(near_grad(k), s_send.at[FAR_GRAD + k])
        whole_wait(lag_send.at[pl.ds(0, part * (seqs // 2))], s_send.at[TERMS_HIGH])

    @pl.when(is_low)
    def _():
        whole_wait(f_all.at[pl.ds(0, half - 1)], s_send.at[TAPS_LOW])
        whole_wait(f_all.at[pl.ds(0, half)], s_send.at[TAPS_CROSS])
        whole_wait(lag_send.at[pl.ds(0, part * (seqs - 1))], s_send.at[TERMS_LOW])

        @pl.when(me // part == seq)
        def _():
            whole_wait(lag_send.at[pl.ds(0, owners - 1)], s_send.at[FINAL])

        @pl.when(me // part != seq)
        def _():
            whole_wait(lag_send, s_send.at[FINAL])


def stay(array):
    return pltpu.with_memory_space_constraint(array, pltpu.HBM)


def per_device(inputs, out_grad, filters, skip):
    channels, tok = inputs.shape[1], inputs.shape[2]
    groups = filters.shape[0]
    owners, seqs = lax.axis_size("context"), lax.axis_size("dp")
    half = owners // 2
    own = groups // half
    blocks = half // 2
    part = owners // seqs
    scale = 1.0 / math.sqrt(seqs * GROUP * tok * owners)
    vmem = pl.BlockSpec(memory_space=pltpu.VMEM)
    hbm = pl.BlockSpec(memory_space=pltpu.HBM)
    tiles = (groups, GROUP, LANES)
    held = (2, own, blocks, GROUP, LANES)
    grad_input, grad_filter = pl.pallas_call(
        functools.partial(kernel, (owners, seqs, scale)),
        out_shape=(
            jax.ShapeDtypeStruct(tiles, BF16),
            jax.ShapeDtypeStruct((groups, LANES), F32),
        ),
        in_specs=[hbm, hbm, hbm, hbm],
        out_specs=(vmem, vmem),
        scratch_shapes=[
            pltpu.VMEM((groups, LANES), F32),
            pltpu.VMEM((channels // LANES, LANES), F32),
            pltpu.VMEM(tiles, BF16),
            pltpu.VMEM((half, own, LANES), F32),
            pltpu.VMEM((owners, own, LANES), F32),
            pltpu.VMEM((2, own, 2 * blocks, GROUP, LANES), BF16),
            pltpu.VMEM((2, own, 3 * blocks, GROUP, LANES), BF16),
            pltpu.VMEM(held, BF16),
            pltpu.VMEM((own, PAIR, blocks * GROUP), BF16),
            pltpu.VMEM((own, LANES, LANES * (owners + 1)), BF16),
            pltpu.VMEM((own, blocks * GROUP, PAIR), F32),
            pltpu.VMEM(held, BF16),
            pltpu.VMEM(tiles, BF16),
            pltpu.VMEM(tiles, F32),
            pltpu.VMEM((own, LANES, LANES * owners), F32),
            pltpu.VMEM((owners, own, LANES), F32),
            pltpu.VMEM((2, seqs, part, own, LANES), F32),
            pltpu.VMEM((part, own, LANES), F32),
            pltpu.VMEM((half, own, LANES), F32),
            pltpu.SemaphoreType.DMA((N_SEMS,)),
            pltpu.SemaphoreType.DMA((N_SEMS,)),
            pltpu.SemaphoreType.DMA((3,)),
            pltpu.SemaphoreType.REGULAR,
        ],
        compiler_params=pltpu.CompilerParams(
            collective_id=0, has_side_effects=True, vmem_limit_bytes=28 * 1024 * 1024),
    )(
        stay(inputs.reshape(tiles)),
        stay(out_grad.reshape(tiles)),
        stay(filters),
        stay(skip.reshape(channels // LANES, LANES)),
    )
    return grad_input.reshape(1, channels, tok), grad_filter


def solution(mesh):
    placed = (
        P("dp", "tensor", "context"),
        P("dp", "tensor", "context"),
        P("tensor", "context"),
        P("tensor"),
    )
    return jax.shard_map(
        per_device,
        mesh=mesh,
        in_specs=placed,
        out_specs=(P("dp", "tensor", "context"), P("tensor", "context")),
        check_vma=False,
    )
```

```python
import functools
import math

import jax
import jax.numpy as jnp
from jax import lax
from jax.experimental import pallas as pl
from jax.experimental.pallas import tpu as pltpu
from jax.sharding import PartitionSpec as P

GROUP = 16
LANES = 128
PAIR = 256
MESH = pl.DeviceIdType.MESH
F32 = jnp.float32
BF16 = jnp.bfloat16

TAPS_LOW, TAPS_HIGH, TAPS_CROSS, BACK, TERMS_LOW, TERMS_HIGH, FINAL = range(7)
NEAR_GRAD, NEAR_IN, FAR_GRAD = 7, 9, 11
N_SEMS = 13


def whole_wait(ref, sem):
    pltpu.make_async_copy(ref, ref, sem).wait()


def kernel(sizes, x_hbm, g_hbm, f_hbm, s_hbm, gi_out, gf_out,
           f_here, s_here, g_here, f_send, f_all, near, far, x_all, turned, toe, acc, back,
           back_all, direct, lag_rows, lag_send, lag_in, lag_fin, gf_all,
           s_send, s_recv, s_loc, ready):
    owners, seqs, scale = sizes
    half = owners // 2
    own = f_send.shape[1]
    blocks = half // 2
    low_taps = half * LANES
    part = owners // seqs
    me = lax.axis_index("context")
    seq = lax.axis_index("dp")
    z, h = me // half, me % half
    core, place = h % 2, h // 2
    is_low, is_high = z == 0, z == 1

    def send(src, dst, k, where):
        pltpu.make_async_remote_copy(
            src_ref=src, dst_ref=dst, send_sem=s_send.at[k], recv_sem=s_recv.at[k],
            device_id=where, device_id_type=MESH).start()

    def local(src, dst, k):
        pltpu.make_async_copy(src, dst, s_recv.at[k]).start()

    def loop(first, body):
        def step(k, carry):
            body((h + k) % half)
            return carry

        lax.fori_loop(first, half, step, 0)

    def signal(where):
        pl.semaphore_signal(barrier, inc=1, device_id=where, device_id_type=MESH)

    barrier = pltpu.get_barrier_semaphore()
    loop(1, lambda o: signal({"context": z * half + o}))

    @pl.when(is_low)
    def _():
        loop(0, lambda o: signal({"context": half + o}))
        for r in range(1, seqs):
            signal({"dp": (seq + r) % seqs})
            signal({"dp": (seq + r) % seqs, "context": half + h})

    stage = [
        pltpu.make_async_copy(f_hbm, f_here, s_loc.at[0]),
        pltpu.make_async_copy(s_hbm, s_here, s_loc.at[1]),
        pltpu.make_async_copy(g_hbm, g_here, s_loc.at[2]),
    ]
    for copy in stage:
        copy.start()
    count = own // 2
    for k in range(2):
        local(g_hbm.at[pl.ds(own * h + count * k, count)],
              near.at[core, pl.ds(count * k, count), place], NEAR_GRAD + k)
        local(x_hbm.at[pl.ds(own * h + count * k, count)],
              x_all.at[core, pl.ds(count * k, count), place], NEAR_IN + k)

    def send_grad(k):
        loop(1, lambda o: send(
            g_hbm.at[pl.ds(own * o + count * k, count)],
            near.at[core, pl.ds(count * k, count), place], NEAR_GRAD + k,
            {"context": z * half + o}))

    def send_in(k):
        loop(1, lambda o: send(
            x_hbm.at[pl.ds(own * o + count * k, count)],
            x_all.at[core, pl.ds(count * k, count), place], NEAR_IN + k,
            {"context": z * half + o}))

    zeros = jnp.zeros((2, own, blocks, GROUP, LANES), BF16)

    stage[0].wait()
    for o in range(half):
        f_send[o] = f_here[own * o : own * (o + 1), :]

    @pl.when(is_high)
    def _():
        pl.semaphore_wait(barrier, half - 1 + half + seqs - 1)
        pl.semaphore_signal(ready, inc=1, device_id={"context": h}, device_id_type=MESH)
        loop(0, lambda o: send(f_send.at[o], f_all.at[me], TAPS_HIGH, {"context": o}))
        loop(0, lambda o: send(
            g_hbm.at[pl.ds(own * o, count)], far.at[core, pl.ds(0, count), blocks + place],
            FAR_GRAD, {"context": o}))
        send_grad(1)
        send_in(1)
        send_grad(0)
        send_in(0)

    @pl.when(is_low)
    def _():
        pl.semaphore_wait(barrier, half - 1 + seqs - 1)
        loop(1, lambda o: send(f_send.at[o], f_all.at[me], TAPS_LOW, {"context": o}))
        local(f_send.at[h], f_all.at[me], TAPS_LOW)
        send_grad(0)
        send_grad(1)
        send_in(0)
        send_in(1)

    near[:, :, blocks:] = zeros

    stage[1].wait()
    stage[2].wait()
    by_row = s_here[...].T
    per = LANES // GROUP
    for m in range(s_here.shape[0]):
        piece = g_here[per * m : per * (m + 1)].reshape(LANES, LANES).astype(F32)
        piece = piece * jnp.broadcast_to(by_row[:, m : m + 1], (LANES, LANES))
        direct[per * m : per * (m + 1)] = piece.reshape(per, GROUP, LANES)

    def build(g, first):
        lead = (
            jnp.zeros((GROUP, LANES), F32) if first == 0
            else jnp.broadcast_to(f_all[first - 1, g : g + 1, :], (GROUP, LANES)))
        rows = jnp.concatenate(
            [lead] + [
                jnp.broadcast_to(f_all[j, g : g + 1, :], (GROUP, LANES))
                for j in range(first, first + half)],
            axis=1)
        row = lax.broadcasted_iota(jnp.int32, rows.shape, 0)
        for bit in (1, 2, 4, 8):
            rows = jnp.where(row % (2 * bit) >= bit, pltpu.roll(rows, bit, 1), rows)
        at = LANES * (first + 1)
        if first == 0:
            toe[g, :, 0:LANES] = jnp.zeros((LANES, LANES), BF16)
        for q in range(LANES // GROUP):
            moved = rows if q == 0 else pltpu.roll(rows, GROUP * q, 1)
            toe[g, GROUP * q : GROUP * (q + 1), at : at + low_taps] = (
                moved[:, LANES:].astype(BF16))

    def rows_of(ref, g, start, count):
        return jnp.concatenate(
            [ref[c, g, start : start + count].reshape(count * GROUP, LANES) for c in range(2)],
            axis=1)

    def against_toe(ref, g, first, last, count):
        left = jnp.concatenate([rows_of(ref, g, d, count) for d in range(first, last)], axis=1)
        lo, hi = PAIR * first, PAIR * last
        right = jnp.concatenate(
            [toe[g, :, LANES + lo : LANES + hi], toe[g, :, lo:hi]], axis=0)
        return lax.dot_general(
            left, right, (((1,), (1,)), ((), ())), preferred_element_type=F32)

    def near_correlation(g):
        step = min(4, blocks)
        for e in range(0, blocks, step):
            count = blocks - e
            term = against_toe(near, g, e, e + step, count)
            if e == 0:
                acc[g] = term
            else:
                acc[g, 0 : count * GROUP] += term

    def far_correlation(g):
        total = acc[g]
        for e in range(0, 2 * blocks, 4):
            total = total + against_toe(far, g, e, e + 4, blocks)
        acc[g] = total

    def send_back(first, count):
        for g in range(first, first + count):
            for c in range(2):
                back[c, g] = acc[g, :, LANES * c : LANES * (c + 1)].astype(BF16).reshape(
                    blocks, GROUP, LANES)
        which = pl.ds(first, count)
        where = pl.ds(own * h + first, count)
        local(back.at[core, which, place], back_all.at[where], BACK)
        loop(1, lambda o: send(
            back.at[o % 2, which, o // 2], back_all.at[where], BACK,
            {"context": z * half + o}))

    def near_lags(g):
        left = jnp.concatenate(
            [x_all[c, g].reshape(blocks * GROUP, LANES).T for c in range(2)], axis=0)
        turned[g] = left
        carry = jnp.zeros((LANES, LANES), F32)
        for d in reversed(range(blocks)):
            square = jnp.dot(left, rows_of(near, g, d, blocks), preferred_element_type=F32)
            at = PAIR * d
            lag_rows[g, :, at : at + LANES] = square[:LANES, :LANES] + square[LANES:, LANES:]
            lag_rows[g, :, at + LANES : at + PAIR] = square[:LANES, LANES:] + carry
            carry = square[LANES:, :LANES]

    def far_lags(g):
        left = turned[g]
        carry = jnp.zeros((LANES, LANES), F32)
        for d in reversed(range(1, 2 * blocks)):
            square = jnp.dot(left, rows_of(far, g, d, blocks), preferred_element_type=F32)
            at = PAIR * d
            even = square[:LANES, :LANES] + square[LANES:, LANES:]
            odd = square[:LANES, LANES:] + carry
            if d < blocks:
                even = even + lag_rows[g, :, at : at + LANES]
                odd = odd + lag_rows[g, :, at + LANES : at + PAIR]
            lag_rows[g, :, at : at + LANES] = even
            lag_rows[g, :, at + LANES : at + PAIR] = odd
            carry = square[LANES:, :LANES]
        lag_rows[g, :, LANES:PAIR] += carry

    def diagonals(g, taps):
        width = taps + LANES
        rows = [
            jnp.concatenate(
                [jnp.zeros((8, LANES), F32), lag_rows[g, 8 * q : 8 * (q + 1), :taps]], axis=1)
            for q in range(LANES // 8)]
        move = 8
        while len(rows) > 1:
            rows = [
                rows[k] + pltpu.roll(rows[k + 1], width - move, 1)
                for k in range(0, len(rows), 2)]
            move = 2 * move
        total = rows[0]
        row = lax.broadcasted_iota(jnp.int32, (8, width), 0)
        for bit in (1, 2, 4):
            total = jnp.where(
                row % (2 * bit) >= bit, pltpu.roll(total, width - bit, 1), total)
        line = jnp.sum(total, axis=0, keepdims=True)[:, LANES:]
        for j in range(taps // LANES):
            lag_send[j, g : g + 1, :] = line[:, LANES * j : LANES * (j + 1)]

    def near_grad(k):
        return near.at[:, pl.ds(count * k, count), pl.ds(0, blocks)]

    def near_in(k):
        return x_all.at[:, pl.ds(count * k, count)]

    def far_grad(k):
        return far.at[:, pl.ds(count * k, count), pl.ds(blocks, blocks)]

    @pl.when(is_high)
    def _():
        whole_wait(near_grad(1), s_recv.at[NEAR_GRAD + 1])
        send(near_grad(1), far_grad(1), FAR_GRAD + 1, {"context": h})
        whole_wait(f_all.at[pl.ds(0, half)], s_recv.at[TAPS_CROSS])
        for g in range(own):
            build(g, 0)
        whole_wait(near_in(1), s_recv.at[NEAR_IN + 1])
        for g in range(count, own):
            near_lags(g)
        for g in range(count, own):
            diagonals(g, low_taps)
        whole_wait(near_grad(0), s_recv.at[NEAR_GRAD])
        for g in range(own):
            near_correlation(g)
        send_back(0, own)
        whole_wait(near_in(0), s_recv.at[NEAR_IN])
        for g in range(count):
            near_lags(g)
        for g in range(count):
            diagonals(g, low_taps)
        for p in range(seqs // 2):
            send(lag_send.at[pl.ds(part * p, part)], lag_in.at[1, seq], TERMS_HIGH,
                 {"dp": p, "context": h})
        whole_wait(back_all, s_recv.at[BACK])

    @pl.when(is_low)
    def _():
        far[:, :, 0:blocks] = zeros
        far[:, :, 2 * blocks :] = zeros
        whole_wait(f_all.at[pl.ds(0, half)], s_recv.at[TAPS_LOW])
        for g in range(own):
            build(g, 0)
        pl.semaphore_wait(ready, 1)
        low = f_all.at[pl.ds(0, half)]
        send(low, low, TAPS_CROSS, {"context": half + h})
        for k in range(2):
            whole_wait(near_grad(k), s_recv.at[NEAR_GRAD + k])
            for g in range(count * k, count * (k + 1)):
                near_correlation(g)
        whole_wait(f_all.at[pl.ds(half, half)], s_recv.at[TAPS_HIGH])
        for g in range(own):
            build(g, half)
        early, late = range(0, count), range(count, own)
        whole_wait(near_in(0), s_recv.at[NEAR_IN])
        for g in early:
            near_lags(g)
        whole_wait(far_grad(0), s_recv.at[FAR_GRAD])
        for g in early:
            far_lags(g)
        for g in early:
            diagonals(g, 2 * low_taps)
        whole_wait(near_in(1), s_recv.at[NEAR_IN + 1])
        for g in late:
            near_lags(g)
        for g in early:
            far_correlation(g)
        send_back(0, count)
        whole_wait(far_grad(1), s_recv.at[FAR_GRAD + 1])
        for g in late:
            far_lags(g)
        for g in late:
            diagonals(g, 2 * low_taps)
        local(lag_send.at[pl.ds(part * seq, part)], lag_in.at[0, seq], TERMS_LOW)
        for r in range(1, seqs):
            p = (seq + r) % seqs
            send(lag_send.at[pl.ds(part * p, part)], lag_in.at[0, seq], TERMS_LOW, {"dp": p})
        for g in late:
            far_correlation(g)
        send_back(count, own - count)

        whole_wait(lag_in.at[0], s_recv.at[TERMS_LOW])
        summed = lag_in[0, 0]
        for b in range(1, seqs):
            summed = summed + lag_in[0, b]
        lag_fin[...] = summed * scale

        @pl.when(seq < seqs // 2)
        def _():
            whole_wait(lag_in.at[1], s_recv.at[TERMS_HIGH])
            more = lag_in[1, 0]
            for b in range(1, seqs):
                more = more + lag_in[1, b]
            lag_fin[...] += more * scale

        def deliver(k, carry):
            at = seq * part + k % part
            to = (seq + k // part) % seqs

            @pl.when((at != me) | (to != seq))
            def _():
                send(lag_fin.at[k % part], gf_all.at[h], FINAL, {"dp": to, "context": at})

            return carry

        lax.fori_loop(0, owners, deliver, 0)

        @pl.when(me // part == seq)
        def _():
            local(lag_fin.at[me % part], gf_all.at[h], FINAL)

        whole_wait(back_all, s_recv.at[BACK])

    gi_out[...] = (back_all[...].astype(F32) + direct[...]).astype(BF16)
    whole_wait(gf_all, s_recv.at[FINAL])
    for o in range(half):
        gf_out[own * o : own * (o + 1), :] = gf_all[o]

    others = own * (half - 1)
    for k in range(2):
        whole_wait(g_hbm.at[pl.ds(0, count * (half - 1))], s_send.at[NEAR_GRAD + k])
        whole_wait(x_hbm.at[pl.ds(0, count * (half - 1))], s_send.at[NEAR_IN + k])
    whole_wait(back_all.at[pl.ds(0, others)], s_send.at[BACK])

    @pl.when(is_high)
    def _():
        whole_wait(f_send, s_send.at[TAPS_HIGH])
        for k in range(2):
            whole_wait(near_grad(k), s_send.at[FAR_GRAD + k])
        whole_wait(lag_send.at[pl.ds(0, part * (seqs // 2))], s_send.at[TERMS_HIGH])

    @pl.when(is_low)
    def _():
        whole_wait(f_all.at[pl.ds(0, half - 1)], s_send.at[TAPS_LOW])
        whole_wait(f_all.at[pl.ds(0, half)], s_send.at[TAPS_CROSS])
        whole_wait(lag_send.at[pl.ds(0, part * (seqs - 1))], s_send.at[TERMS_LOW])

        @pl.when(me // part == seq)
        def _():
            whole_wait(lag_send.at[pl.ds(0, owners - 1)], s_send.at[FINAL])

        @pl.when(me // part != seq)
        def _():
            whole_wait(lag_send, s_send.at[FINAL])


def stay(array):
    return pltpu.with_memory_space_constraint(array, pltpu.HBM)


def per_device(inputs, out_grad, filters, skip):
    channels, tok = inputs.shape[1], inputs.shape[2]
    groups = filters.shape[0]
    owners, seqs = lax.axis_size("context"), lax.axis_size("dp")
    half = owners // 2
    own = groups // half
    blocks = half // 2
    part = owners // seqs
    scale = 1.0 / math.sqrt(seqs * GROUP * tok * owners)
    vmem = pl.BlockSpec(memory_space=pltpu.VMEM)
    hbm = pl.BlockSpec(memory_space=pltpu.HBM)
    tiles = (groups, GROUP, LANES)
    held = (2, own, blocks, GROUP, LANES)
    grad_input, grad_filter = pl.pallas_call(
        functools.partial(kernel, (owners, seqs, scale)),
        out_shape=(
            jax.ShapeDtypeStruct(tiles, BF16),
            jax.ShapeDtypeStruct((groups, LANES), F32),
        ),
        in_specs=[hbm, hbm, hbm, hbm],
        out_specs=(vmem, vmem),
        scratch_shapes=[
            pltpu.VMEM((groups, LANES), F32),
            pltpu.VMEM((channels // LANES, LANES), F32),
            pltpu.VMEM(tiles, BF16),
            pltpu.VMEM((half, own, LANES), F32),
            pltpu.VMEM((owners, own, LANES), F32),
            pltpu.VMEM((2, own, 2 * blocks, GROUP, LANES), BF16),
            pltpu.VMEM((2, own, 3 * blocks, GROUP, LANES), BF16),
            pltpu.VMEM(held, BF16),
            pltpu.VMEM((own, PAIR, blocks * GROUP), BF16),
            pltpu.VMEM((own, LANES, LANES * (owners + 1)), BF16),
            pltpu.VMEM((own, blocks * GROUP, PAIR), F32),
            pltpu.VMEM(held, BF16),
            pltpu.VMEM(tiles, BF16),
            pltpu.VMEM(tiles, F32),
            pltpu.VMEM((own, LANES, LANES * owners), F32),
            pltpu.VMEM((owners, own, LANES), F32),
            pltpu.VMEM((2, seqs, part, own, LANES), F32),
            pltpu.VMEM((part, own, LANES), F32),
            pltpu.VMEM((half, own, LANES), F32),
            pltpu.SemaphoreType.DMA((N_SEMS,)),
            pltpu.SemaphoreType.DMA((N_SEMS,)),
            pltpu.SemaphoreType.DMA((3,)),
            pltpu.SemaphoreType.REGULAR,
        ],
        compiler_params=pltpu.CompilerParams(
            collective_id=0, has_side_effects=True, vmem_limit_bytes=28 * 1024 * 1024),
    )(
        stay(inputs.reshape(tiles)),
        stay(out_grad.reshape(tiles)),
        stay(filters),
        stay(skip.reshape(channels // LANES, LANES)),
    )
    return grad_input.reshape(1, channels, tok), grad_filter


def solution(mesh):
    placed = (
        P("dp", "tensor", "context"),
        P("dp", "tensor", "context"),
        P("tensor", "context"),
        P("tensor"),
    )
    return jax.shard_map(
        per_device,
        mesh=mesh,
        in_specs=placed,
        out_specs=(P("dp", "tensor", "context"), P("tensor", "context")),
        check_vma=False,
    )
```

```python
import functools
import math

import jax
import jax.numpy as jnp
from jax import lax
from jax.experimental import pallas as pl
from jax.experimental.pallas import tpu as pltpu
from jax.sharding import PartitionSpec as P

GROUP = 16
LANES = 128
PAIR = 256
MESH = pl.DeviceIdType.MESH
F32 = jnp.float32
BF16 = jnp.bfloat16

TAPS_LOW, TAPS_HIGH, TAPS_CROSS, BACK, TERMS_LOW, TERMS_HIGH, FINAL = range(7)
NEAR_GRAD, NEAR_IN, FAR_GRAD = 7, 9, 11
N_SEMS = 14


def whole_wait(ref, sem):
    pltpu.make_async_copy(ref, ref, sem).wait()


def kernel(sizes, x_hbm, g_hbm, f_hbm, s_hbm, gi_out, gf_out,
           f_here, s_here, g_here, f_send, f_all, near, far, x_all, turned, toe, acc, back,
           back_all, direct, lag_rows, lag_send, lag_in, lag_fin, gf_all,
           s_send, s_recv, s_loc, ready):
    owners, seqs, scale = sizes
    half = owners // 2
    own = f_send.shape[1]
    blocks = half // 2
    low_taps = half * LANES
    part = owners // seqs
    me = lax.axis_index("context")
    seq = lax.axis_index("dp")
    z, h = me // half, me % half
    core, place = h % 2, h // 2
    is_low, is_high = z == 0, z == 1

    def send(src, dst, k, where):
        pltpu.make_async_remote_copy(
            src_ref=src, dst_ref=dst, send_sem=s_send.at[k], recv_sem=s_recv.at[k],
            device_id=where, device_id_type=MESH).start()

    def local(src, dst, k):
        pltpu.make_async_copy(src, dst, s_recv.at[k]).start()

    def loop(first, body):
        def step(k, carry):
            body((h + k) % half)
            return carry

        lax.fori_loop(first, half, step, 0)

    def signal(where):
        pl.semaphore_signal(barrier, inc=1, device_id=where, device_id_type=MESH)

    stage = [
        pltpu.make_async_copy(f_hbm, f_here, s_loc.at[0]),
        pltpu.make_async_copy(s_hbm, s_here, s_loc.at[1]),
        pltpu.make_async_copy(g_hbm, g_here, s_loc.at[2]),
    ]
    for copy in stage:
        copy.start()

    barrier = pltpu.get_barrier_semaphore()
    loop(1, lambda o: signal({"context": z * half + o}))

    @pl.when(is_low)
    def _():
        loop(0, lambda o: signal({"context": half + o}))
        for r in range(1, seqs):
            signal({"dp": (seq + r) % seqs})
            signal({"dp": (seq + r) % seqs, "context": half + h})

    count = own // 2
    for k in range(2):
        local(g_hbm.at[pl.ds(own * h + count * k, count)],
              near.at[core, pl.ds(count * k, count), place], NEAR_GRAD + k)
        local(x_hbm.at[pl.ds(own * h + count * k, count)],
              x_all.at[core, pl.ds(count * k, count), place], NEAR_IN + k)

    def send_grad(k):
        loop(1, lambda o: send(
            g_hbm.at[pl.ds(own * o + count * k, count)],
            near.at[core, pl.ds(count * k, count), place], NEAR_GRAD + k,
            {"context": z * half + o}))

    def send_in(k):
        loop(1, lambda o: send(
            x_hbm.at[pl.ds(own * o + count * k, count)],
            x_all.at[core, pl.ds(count * k, count), place], NEAR_IN + k,
            {"context": z * half + o}))

    zeros = jnp.zeros((2, own, blocks, GROUP, LANES), BF16)

    stage[0].wait()
    for o in range(half):
        f_send[o] = f_here[own * o : own * (o + 1), :]

    @pl.when(is_high)
    def _():
        pl.semaphore_wait(barrier, half - 1 + half + seqs - 1)
        pl.semaphore_signal(ready, inc=1, device_id={"context": h}, device_id_type=MESH)
        loop(0, lambda o: send(f_send.at[o], f_all.at[me], TAPS_HIGH, {"context": o}))
        loop(0, lambda o: send(
            g_hbm.at[pl.ds(own * o, count)], far.at[core, pl.ds(0, count), blocks + place],
            FAR_GRAD, {"context": o}))
        send_grad(1)
        send_in(1)
        send_grad(0)
        send_in(0)

    @pl.when(is_low)
    def _():
        pl.semaphore_wait(barrier, half - 1 + seqs - 1)
        loop(1, lambda o: send(f_send.at[o], f_all.at[me], TAPS_LOW, {"context": o}))
        local(f_send.at[h], f_all.at[me], TAPS_LOW)
        send_grad(0)
        send_grad(1)
        send_in(0)
        send_in(1)

    near[:, :, blocks:] = zeros

    stage[1].wait()
    stage[2].wait()
    by_row = s_here[...].T
    per = LANES // GROUP
    for m in range(s_here.shape[0]):
        piece = g_here[per * m : per * (m + 1)].reshape(LANES, LANES).astype(F32)
        piece = piece * jnp.broadcast_to(by_row[:, m : m + 1], (LANES, LANES))
        direct[per * m : per * (m + 1)] = piece.reshape(per, GROUP, LANES)

    def build(g, first):
        lead = (
            jnp.zeros((GROUP, LANES), F32) if first == 0
            else jnp.broadcast_to(f_all[first - 1, g : g + 1, :], (GROUP, LANES)))
        rows = jnp.concatenate(
            [lead] + [
                jnp.broadcast_to(f_all[j, g : g + 1, :], (GROUP, LANES))
                for j in range(first, first + half)],
            axis=1)
        row = lax.broadcasted_iota(jnp.int32, rows.shape, 0)
        for bit in (1, 2, 4, 8):
            rows = jnp.where(row % (2 * bit) >= bit, pltpu.roll(rows, bit, 1), rows)
        at = LANES * (first + 1)
        if first == 0:
            toe[g, :, 0:LANES] = jnp.zeros((LANES, LANES), BF16)
        for q in range(LANES // GROUP):
            moved = rows if q == 0 else pltpu.roll(rows, GROUP * q, 1)
            toe[g, GROUP * q : GROUP * (q + 1), at : at + low_taps] = (
                moved[:, LANES:].astype(BF16))

    def rows_of(ref, g, start, count):
        return jnp.concatenate(
            [ref[c, g, start : start + count].reshape(count * GROUP, LANES) for c in range(2)],
            axis=1)

    def against_toe(ref, g, first, last, count):
        left = jnp.concatenate([rows_of(ref, g, d, count) for d in range(first, last)], axis=1)
        lo, hi = PAIR * first, PAIR * last
        right = jnp.concatenate(
            [toe[g, :, LANES + lo : LANES + hi], toe[g, :, lo:hi]], axis=0)
        return lax.dot_general(
            left, right, (((1,), (1,)), ((), ())), preferred_element_type=F32)

    def near_correlation(g):
        step = min(4, blocks)
        for e in range(0, blocks, step):
            count = blocks - e
            term = against_toe(near, g, e, e + step, count)
            if e == 0:
                acc[g] = term
            else:
                acc[g, 0 : count * GROUP] += term

    def far_correlation(g):
        total = acc[g]
        for e in range(0, 2 * blocks, 4):
            total = total + against_toe(far, g, e, e + 4, blocks)
        acc[g] = total

    def send_back(first, count):
        for g in range(first, first + count):
            for c in range(2):
                back[c, g] = acc[g, :, LANES * c : LANES * (c + 1)].astype(BF16).reshape(
                    blocks, GROUP, LANES)
        which = pl.ds(first, count)
        where = pl.ds(own * h + first, count)
        local(back.at[core, which, place], back_all.at[where], BACK)
        loop(1, lambda o: send(
            back.at[o % 2, which, o // 2], back_all.at[where], BACK,
            {"context": z * half + o}))

    def near_lags(g):
        left = jnp.concatenate(
            [x_all[c, g].reshape(blocks * GROUP, LANES).T for c in range(2)], axis=0)
        turned[g] = left
        carry = jnp.zeros((LANES, LANES), F32)
        for d in reversed(range(blocks)):
            square = jnp.dot(left, rows_of(near, g, d, blocks), preferred_element_type=F32)
            at = PAIR * d
            lag_rows[g, :, at : at + LANES] = square[:LANES, :LANES] + square[LANES:, LANES:]
            lag_rows[g, :, at + LANES : at + PAIR] = square[:LANES, LANES:] + carry
            carry = square[LANES:, :LANES]

    def far_lags(g):
        left = turned[g]
        carry = jnp.zeros((LANES, LANES), F32)
        for d in reversed(range(1, 2 * blocks)):
            square = jnp.dot(left, rows_of(far, g, d, blocks), preferred_element_type=F32)
            at = PAIR * d
            even = square[:LANES, :LANES] + square[LANES:, LANES:]
            odd = square[:LANES, LANES:] + carry
            if d < blocks:
                even = even + lag_rows[g, :, at : at + LANES]
                odd = odd + lag_rows[g, :, at + LANES : at + PAIR]
            lag_rows[g, :, at : at + LANES] = even
            lag_rows[g, :, at + LANES : at + PAIR] = odd
            carry = square[LANES:, :LANES]
        lag_rows[g, :, LANES:PAIR] += carry

    def diagonals(g, taps):
        width = taps + LANES
        rows = [
            jnp.concatenate(
                [jnp.zeros((8, LANES), F32), lag_rows[g, 8 * q : 8 * (q + 1), :taps]], axis=1)
            for q in range(LANES // 8)]
        move = 8
        while len(rows) > 1:
            rows = [
                rows[k] + pltpu.roll(rows[k + 1], width - move, 1)
                for k in range(0, len(rows), 2)]
            move = 2 * move
        total = rows[0]
        row = lax.broadcasted_iota(jnp.int32, (8, width), 0)
        for bit in (1, 2, 4):
            total = jnp.where(
                row % (2 * bit) >= bit, pltpu.roll(total, width - bit, 1), total)
        line = jnp.sum(total, axis=0, keepdims=True)[:, LANES:]
        for j in range(taps // LANES):
            lag_send[j, g : g + 1, :] = line[:, LANES * j : LANES * (j + 1)]

    def near_grad(k):
        return near.at[:, pl.ds(count * k, count), pl.ds(0, blocks)]

    def near_in(k):
        return x_all.at[:, pl.ds(count * k, count)]

    def far_grad(g, n):
        return far.at[:, pl.ds(g, n), pl.ds(blocks, blocks)]

    @pl.when(is_high)
    def _():
        whole_wait(near_grad(1), s_recv.at[NEAR_GRAD + 1])
        for g in range(count, own):
            send(near.at[:, pl.ds(g, 1), pl.ds(0, blocks)], far_grad(g, 1),
                 FAR_GRAD + 1 + g - count, {"context": h})
        whole_wait(f_all.at[pl.ds(0, half)], s_recv.at[TAPS_CROSS])
        for g in range(own):
            build(g, 0)
        whole_wait(near_in(1), s_recv.at[NEAR_IN + 1])
        for g in range(count, own):
            near_lags(g)
        for g in range(count, own):
            diagonals(g, low_taps)
        whole_wait(near_grad(0), s_recv.at[NEAR_GRAD])
        for g in range(own):
            near_correlation(g)
        send_back(0, own)
        whole_wait(near_in(0), s_recv.at[NEAR_IN])
        for g in range(count):
            near_lags(g)
        for g in range(count):
            diagonals(g, low_taps)
        for p in range(seqs // 2):
            send(lag_send.at[pl.ds(part * p, part)], lag_in.at[1, seq], TERMS_HIGH,
                 {"dp": p, "context": h})
        whole_wait(back_all, s_recv.at[BACK])

    @pl.when(is_low)
    def _():
        far[:, :, 0:blocks] = zeros
        far[:, :, 2 * blocks :] = zeros
        whole_wait(f_all.at[pl.ds(0, half)], s_recv.at[TAPS_LOW])
        for g in range(own):
            build(g, 0)
        pl.semaphore_wait(ready, 1)
        low = f_all.at[pl.ds(0, half)]
        send(low, low, TAPS_CROSS, {"context": half + h})
        for k in range(2):
            whole_wait(near_grad(k), s_recv.at[NEAR_GRAD + k])
            for g in range(count * k, count * (k + 1)):
                near_correlation(g)
        whole_wait(f_all.at[pl.ds(half, half)], s_recv.at[TAPS_HIGH])
        for g in range(own):
            build(g, half)
        early, late = range(0, count), range(count, own)
        whole_wait(near_in(0), s_recv.at[NEAR_IN])
        for g in early:
            near_lags(g)
        whole_wait(far_grad(0, count), s_recv.at[FAR_GRAD])
        for g in early:
            far_lags(g)
        for g in early:
            diagonals(g, 2 * low_taps)
        whole_wait(near_in(1), s_recv.at[NEAR_IN + 1])
        for g in late:
            near_lags(g)
        for g in early:
            far_correlation(g)
        send_back(0, count)
        for g in late:
            whole_wait(far_grad(g, 1), s_recv.at[FAR_GRAD + 1 + g - count])
            far_lags(g)
            diagonals(g, 2 * low_taps)
        local(lag_send.at[pl.ds(part * seq, part)], lag_in.at[0, seq], TERMS_LOW)
        for r in range(1, seqs):
            p = (seq + r) % seqs
            send(lag_send.at[pl.ds(part * p, part)], lag_in.at[0, seq], TERMS_LOW, {"dp": p})
        for g in late:
            far_correlation(g)
        send_back(count, own - count)

        whole_wait(lag_in.at[0], s_recv.at[TERMS_LOW])
        summed = lag_in[0, 0]
        for b in range(1, seqs):
            summed = summed + lag_in[0, b]
        lag_fin[...] = summed * scale

        @pl.when(seq < seqs // 2)
        def _():
            whole_wait(lag_in.at[1], s_recv.at[TERMS_HIGH])
            more = lag_in[1, 0]
            for b in range(1, seqs):
                more = more + lag_in[1, b]
            lag_fin[...] += more * scale

        def deliver(k, carry):
            at = seq * part + k % part
            to = (seq + k // part) % seqs

            @pl.when((at != me) | (to != seq))
            def _():
                send(lag_fin.at[k % part], gf_all.at[h], FINAL, {"dp": to, "context": at})

            return carry

        lax.fori_loop(0, owners, deliver, 0)

        @pl.when(me // part == seq)
        def _():
            local(lag_fin.at[me % part], gf_all.at[h], FINAL)

        whole_wait(back_all, s_recv.at[BACK])

    gi_out[...] = (back_all[...].astype(F32) + direct[...]).astype(BF16)
    whole_wait(gf_all, s_recv.at[FINAL])
    for o in range(half):
        gf_out[own * o : own * (o + 1), :] = gf_all[o]

    others = own * (half - 1)
    for k in range(2):
        whole_wait(g_hbm.at[pl.ds(0, count * (half - 1))], s_send.at[NEAR_GRAD + k])
        whole_wait(x_hbm.at[pl.ds(0, count * (half - 1))], s_send.at[NEAR_IN + k])
    whole_wait(back_all.at[pl.ds(0, others)], s_send.at[BACK])

    @pl.when(is_high)
    def _():
        whole_wait(f_send, s_send.at[TAPS_HIGH])
        whole_wait(near_grad(0), s_send.at[FAR_GRAD])
        for g in range(count, own):
            whole_wait(far_grad(g, 1), s_send.at[FAR_GRAD + 1 + g - count])
        whole_wait(lag_send.at[pl.ds(0, part * (seqs // 2))], s_send.at[TERMS_HIGH])

    @pl.when(is_low)
    def _():
        whole_wait(f_all.at[pl.ds(0, half - 1)], s_send.at[TAPS_LOW])
        whole_wait(f_all.at[pl.ds(0, half)], s_send.at[TAPS_CROSS])
        whole_wait(lag_send.at[pl.ds(0, part * (seqs - 1))], s_send.at[TERMS_LOW])

        @pl.when(me // part == seq)
        def _():
            whole_wait(lag_send.at[pl.ds(0, owners - 1)], s_send.at[FINAL])

        @pl.when(me // part != seq)
        def _():
            whole_wait(lag_send, s_send.at[FINAL])


def stay(array):
    return pltpu.with_memory_space_constraint(array, pltpu.HBM)


def per_device(inputs, out_grad, filters, skip):
    channels, tok = inputs.shape[1], inputs.shape[2]
    groups = filters.shape[0]
    owners, seqs = lax.axis_size("context"), lax.axis_size("dp")
    half = owners // 2
    own = groups // half
    blocks = half // 2
    part = owners // seqs
    scale = 1.0 / math.sqrt(seqs * GROUP * tok * owners)
    vmem = pl.BlockSpec(memory_space=pltpu.VMEM)
    hbm = pl.BlockSpec(memory_space=pltpu.HBM)
    tiles = (groups, GROUP, LANES)
    held = (2, own, blocks, GROUP, LANES)
    grad_input, grad_filter = pl.pallas_call(
        functools.partial(kernel, (owners, seqs, scale)),
        out_shape=(
            jax.ShapeDtypeStruct(tiles, BF16),
            jax.ShapeDtypeStruct((groups, LANES), F32),
        ),
        in_specs=[hbm, hbm, hbm, hbm],
        out_specs=(vmem, vmem),
        scratch_shapes=[
            pltpu.VMEM((groups, LANES), F32),
            pltpu.VMEM((channels // LANES, LANES), F32),
            pltpu.VMEM(tiles, BF16),
            pltpu.VMEM((half, own, LANES), F32),
            pltpu.VMEM((owners, own, LANES), F32),
            pltpu.VMEM((2, own, 2 * blocks, GROUP, LANES), BF16),
            pltpu.VMEM((2, own, 3 * blocks, GROUP, LANES), BF16),
            pltpu.VMEM(held, BF16),
            pltpu.VMEM((own, PAIR, blocks * GROUP), BF16),
            pltpu.VMEM((own, LANES, LANES * (owners + 1)), BF16),
            pltpu.VMEM((own, blocks * GROUP, PAIR), F32),
            pltpu.VMEM(held, BF16),
            pltpu.VMEM(tiles, BF16),
            pltpu.VMEM(tiles, F32),
            pltpu.VMEM((own, LANES, LANES * owners), F32),
            pltpu.VMEM((owners, own, LANES), F32),
            pltpu.VMEM((2, seqs, part, own, LANES), F32),
            pltpu.VMEM((part, own, LANES), F32),
            pltpu.VMEM((half, own, LANES), F32),
            pltpu.SemaphoreType.DMA((N_SEMS,)),
            pltpu.SemaphoreType.DMA((N_SEMS,)),
            pltpu.SemaphoreType.DMA((3,)),
            pltpu.SemaphoreType.REGULAR,
        ],
        compiler_params=pltpu.CompilerParams(
            collective_id=0, has_side_effects=True, vmem_limit_bytes=28 * 1024 * 1024),
    )(
        stay(inputs.reshape(tiles)),
        stay(out_grad.reshape(tiles)),
        stay(filters),
        stay(skip.reshape(channels // LANES, LANES)),
    )
    return grad_input.reshape(1, channels, tok), grad_filter


def solution(mesh):
    placed = (
        P("dp", "tensor", "context"),
        P("dp", "tensor", "context"),
        P("tensor", "context"),
        P("tensor"),
    )
    return jax.shard_map(
        per_device,
        mesh=mesh,
        in_specs=placed,
        out_specs=(P("dp", "tensor", "context"), P("tensor", "context")),
        check_vma=False,
    )
```

```python
import functools
import math

import jax
import jax.numpy as jnp
from jax import lax
from jax.experimental import pallas as pl
from jax.experimental.pallas import tpu as pltpu
from jax.sharding import PartitionSpec as P

GROUP = 16
LANES = 128
PAIR = 256
MESH = pl.DeviceIdType.MESH
F32 = jnp.float32
BF16 = jnp.bfloat16

TAPS_LOW, TAPS_HIGH, TAPS_CROSS, BACK, TERMS_LOW, TERMS_HIGH, FINAL = range(7)
NEAR_GRAD, NEAR_IN, FAR_GRAD = 7, 9, 11
N_SEMS = 14


def whole_wait(ref, sem):
    pltpu.make_async_copy(ref, ref, sem).wait()


def kernel(sizes, x_hbm, g_hbm, f_hbm, s_hbm, gi_out, gf_out,
           f_here, s_here, g_here, f_send, f_all, near, far, x_all, turned, toe, acc, back,
           back_all, direct, lag_rows, lag_send, lag_in, lag_fin, gf_all,
           s_send, s_recv, s_loc, ready):
    owners, seqs, scale = sizes
    half = owners // 2
    own = f_send.shape[1]
    blocks = half // 2
    low_taps = half * LANES
    part = owners // seqs
    me = lax.axis_index("context")
    seq = lax.axis_index("dp")
    z, h = me // half, me % half
    core, place = h % 2, h // 2
    is_low, is_high = z == 0, z == 1

    def send(src, dst, k, where):
        pltpu.make_async_remote_copy(
            src_ref=src, dst_ref=dst, send_sem=s_send.at[k], recv_sem=s_recv.at[k],
            device_id=where, device_id_type=MESH).start()

    def local(src, dst, k):
        pltpu.make_async_copy(src, dst, s_recv.at[k]).start()

    def loop(first, body):
        def step(k, carry):
            away = half // 2 + (k + 1) // 2 * (2 * (k % 2) - 1)
            body((h + away) % half)
            return carry

        lax.fori_loop(0, half - first, step, 0)

    def signal(where):
        pl.semaphore_signal(barrier, inc=1, device_id=where, device_id_type=MESH)

    stage = [
        pltpu.make_async_copy(f_hbm, f_here, s_loc.at[0]),
        pltpu.make_async_copy(s_hbm, s_here, s_loc.at[1]),
        pltpu.make_async_copy(g_hbm, g_here, s_loc.at[2]),
    ]
    for copy in stage:
        copy.start()

    barrier = pltpu.get_barrier_semaphore()
    loop(1, lambda o: signal({"context": z * half + o}))

    @pl.when(is_low)
    def _():
        loop(0, lambda o: signal({"context": half + o}))
        for r in range(1, seqs):
            signal({"dp": (seq + r) % seqs})
            signal({"dp": (seq + r) % seqs, "context": half + h})

    count = own // 2
    for k in range(2):
        local(g_hbm.at[pl.ds(own * h + count * k, count)],
              near.at[core, pl.ds(count * k, count), place], NEAR_GRAD + k)
        local(x_hbm.at[pl.ds(own * h + count * k, count)],
              x_all.at[core, pl.ds(count * k, count), place], NEAR_IN + k)

    def send_grad(k):
        loop(1, lambda o: send(
            g_hbm.at[pl.ds(own * o + count * k, count)],
            near.at[core, pl.ds(count * k, count), place], NEAR_GRAD + k,
            {"context": z * half + o}))

    def send_in(k):
        loop(1, lambda o: send(
            x_hbm.at[pl.ds(own * o + count * k, count)],
            x_all.at[core, pl.ds(count * k, count), place], NEAR_IN + k,
            {"context": z * half + o}))

    zeros = jnp.zeros((2, own, blocks, GROUP, LANES), BF16)

    stage[0].wait()
    for o in range(half):
        f_send[o] = f_here[own * o : own * (o + 1), :]

    @pl.when(is_high)
    def _():
        pl.semaphore_wait(barrier, half - 1 + half + seqs - 1)
        pl.semaphore_signal(ready, inc=1, device_id={"context": h}, device_id_type=MESH)
        loop(0, lambda o: send(f_send.at[o], f_all.at[me], TAPS_HIGH, {"context": o}))
        loop(0, lambda o: send(
            g_hbm.at[pl.ds(own * o, count)], far.at[core, pl.ds(0, count), blocks + place],
            FAR_GRAD, {"context": o}))
        send_grad(1)
        send_in(1)
        send_grad(0)
        send_in(0)

    @pl.when(is_low)
    def _():
        pl.semaphore_wait(barrier, half - 1 + seqs - 1)
        loop(1, lambda o: send(f_send.at[o], f_all.at[me], TAPS_LOW, {"context": o}))
        local(f_send.at[h], f_all.at[me], TAPS_LOW)
        send_grad(0)
        send_grad(1)
        send_in(0)
        send_in(1)

    near[:, :, blocks:] = zeros

    stage[1].wait()
    stage[2].wait()
    by_row = s_here[...].T
    per = LANES // GROUP
    for m in range(s_here.shape[0]):
        piece = g_here[per * m : per * (m + 1)].reshape(LANES, LANES).astype(F32)
        piece = piece * jnp.broadcast_to(by_row[:, m : m + 1], (LANES, LANES))
        direct[per * m : per * (m + 1)] = piece.reshape(per, GROUP, LANES)

    def build(g, first):
        lead = (
            jnp.zeros((GROUP, LANES), F32) if first == 0
            else jnp.broadcast_to(f_all[first - 1, g : g + 1, :], (GROUP, LANES)))
        rows = jnp.concatenate(
            [lead] + [
                jnp.broadcast_to(f_all[j, g : g + 1, :], (GROUP, LANES))
                for j in range(first, first + half)],
            axis=1)
        row = lax.broadcasted_iota(jnp.int32, rows.shape, 0)
        for bit in (1, 2, 4, 8):
            rows = jnp.where(row % (2 * bit) >= bit, pltpu.roll(rows, bit, 1), rows)
        at = LANES * (first + 1)
        if first == 0:
            toe[g, :, 0:LANES] = jnp.zeros((LANES, LANES), BF16)
        for q in range(LANES // GROUP):
            moved = rows if q == 0 else pltpu.roll(rows, GROUP * q, 1)
            toe[g, GROUP * q : GROUP * (q + 1), at : at + low_taps] = (
                moved[:, LANES:].astype(BF16))

    def rows_of(ref, g, start, count):
        return jnp.concatenate(
            [ref[c, g, start : start + count].reshape(count * GROUP, LANES) for c in range(2)],
            axis=1)

    def against_toe(ref, g, first, last, count):
        left = jnp.concatenate([rows_of(ref, g, d, count) for d in range(first, last)], axis=1)
        lo, hi = PAIR * first, PAIR * last
        right = jnp.concatenate(
            [toe[g, :, LANES + lo : LANES + hi], toe[g, :, lo:hi]], axis=0)
        return lax.dot_general(
            left, right, (((1,), (1,)), ((), ())), preferred_element_type=F32)

    def near_correlation(g):
        step = min(4, blocks)
        for e in range(0, blocks, step):
            count = blocks - e
            term = against_toe(near, g, e, e + step, count)
            if e == 0:
                acc[g] = term
            else:
                acc[g, 0 : count * GROUP] += term

    def far_correlation(g):
        total = acc[g]
        for e in range(0, 2 * blocks, 4):
            total = total + against_toe(far, g, e, e + 4, blocks)
        acc[g] = total

    def send_back(first, count):
        for g in range(first, first + count):
            for c in range(2):
                back[c, g] = acc[g, :, LANES * c : LANES * (c + 1)].astype(BF16).reshape(
                    blocks, GROUP, LANES)
        which = pl.ds(first, count)
        where = pl.ds(own * h + first, count)
        local(back.at[core, which, place], back_all.at[where], BACK)
        loop(1, lambda o: send(
            back.at[o % 2, which, o // 2], back_all.at[where], BACK,
            {"context": z * half + o}))

    def near_lags(g):
        left = jnp.concatenate(
            [x_all[c, g].reshape(blocks * GROUP, LANES).T for c in range(2)], axis=0)
        turned[g] = left
        carry = jnp.zeros((LANES, LANES), F32)
        for d in reversed(range(blocks)):
            square = jnp.dot(left, rows_of(near, g, d, blocks), preferred_element_type=F32)
            at = PAIR * d
            lag_rows[g, :, at : at + LANES] = square[:LANES, :LANES] + square[LANES:, LANES:]
            lag_rows[g, :, at + LANES : at + PAIR] = square[:LANES, LANES:] + carry
            carry = square[LANES:, :LANES]

    def far_lags(g):
        left = turned[g]
        carry = jnp.zeros((LANES, LANES), F32)
        for d in reversed(range(1, 2 * blocks)):
            square = jnp.dot(left, rows_of(far, g, d, blocks), preferred_element_type=F32)
            at = PAIR * d
            even = square[:LANES, :LANES] + square[LANES:, LANES:]
            odd = square[:LANES, LANES:] + carry
            if d < blocks:
                even = even + lag_rows[g, :, at : at + LANES]
                odd = odd + lag_rows[g, :, at + LANES : at + PAIR]
            lag_rows[g, :, at : at + LANES] = even
            lag_rows[g, :, at + LANES : at + PAIR] = odd
            carry = square[LANES:, :LANES]
        lag_rows[g, :, LANES:PAIR] += carry

    def diagonals(g, taps):
        width = taps + LANES
        rows = [
            jnp.concatenate(
                [jnp.zeros((8, LANES), F32), lag_rows[g, 8 * q : 8 * (q + 1), :taps]], axis=1)
            for q in range(LANES // 8)]
        move = 8
        while len(rows) > 1:
            rows = [
                rows[k] + pltpu.roll(rows[k + 1], width - move, 1)
                for k in range(0, len(rows), 2)]
            move = 2 * move
        total = rows[0]
        row = lax.broadcasted_iota(jnp.int32, (8, width), 0)
        for bit in (1, 2, 4):
            total = jnp.where(
                row % (2 * bit) >= bit, pltpu.roll(total, width - bit, 1), total)
        line = jnp.sum(total, axis=0, keepdims=True)[:, LANES:]
        for j in range(taps // LANES):
            lag_send[j, g : g + 1, :] = line[:, LANES * j : LANES * (j + 1)]

    def near_grad(k):
        return near.at[:, pl.ds(count * k, count), pl.ds(0, blocks)]

    def near_in(k):
        return x_all.at[:, pl.ds(count * k, count)]

    def far_grad(g, n):
        return far.at[:, pl.ds(g, n), pl.ds(blocks, blocks)]

    @pl.when(is_high)
    def _():
        whole_wait(near_grad(1), s_recv.at[NEAR_GRAD + 1])
        for g in range(count, own):
            send(near.at[:, pl.ds(g, 1), pl.ds(0, blocks)], far_grad(g, 1),
                 FAR_GRAD + 1 + g - count, {"context": h})
        whole_wait(f_all.at[pl.ds(0, half)], s_recv.at[TAPS_CROSS])
        for g in range(own):
            build(g, 0)
        whole_wait(near_in(1), s_recv.at[NEAR_IN + 1])
        for g in range(count, own):
            near_lags(g)
        for g in range(count, own):
            diagonals(g, low_taps)
        whole_wait(near_grad(0), s_recv.at[NEAR_GRAD])
        for g in range(own):
            near_correlation(g)
        send_back(0, own)
        whole_wait(near_in(0), s_recv.at[NEAR_IN])
        for g in range(count):
            near_lags(g)
        for g in range(count):
            diagonals(g, low_taps)
        for p in range(seqs // 2):
            send(lag_send.at[pl.ds(part * p, part)], lag_in.at[1, seq], TERMS_HIGH,
                 {"dp": p, "context": h})
        whole_wait(back_all, s_recv.at[BACK])

    @pl.when(is_low)
    def _():
        far[:, :, 0:blocks] = zeros
        far[:, :, 2 * blocks :] = zeros
        whole_wait(f_all.at[pl.ds(0, half)], s_recv.at[TAPS_LOW])
        for g in range(own):
            build(g, 0)
        pl.semaphore_wait(ready, 1)
        low = f_all.at[pl.ds(0, half)]
        send(low, low, TAPS_CROSS, {"context": half + h})
        for k in range(2):
            whole_wait(near_grad(k), s_recv.at[NEAR_GRAD + k])
            for g in range(count * k, count * (k + 1)):
                near_correlation(g)
        whole_wait(f_all.at[pl.ds(half, half)], s_recv.at[TAPS_HIGH])
        for g in range(own):
            build(g, half)
        early, late = range(0, count), range(count, own)
        whole_wait(near_in(0), s_recv.at[NEAR_IN])
        for g in early:
            near_lags(g)
        whole_wait(far_grad(0, count), s_recv.at[FAR_GRAD])
        for g in early:
            far_lags(g)
        for g in early:
            diagonals(g, 2 * low_taps)
        whole_wait(near_in(1), s_recv.at[NEAR_IN + 1])
        for g in late:
            near_lags(g)
        for g in early:
            far_correlation(g)
        send_back(0, count)
        for g in late:
            whole_wait(far_grad(g, 1), s_recv.at[FAR_GRAD + 1 + g - count])
            far_lags(g)
            diagonals(g, 2 * low_taps)
        local(lag_send.at[pl.ds(part * seq, part)], lag_in.at[0, seq], TERMS_LOW)
        for r in range(1, seqs):
            p = (seq + r) % seqs
            send(lag_send.at[pl.ds(part * p, part)], lag_in.at[0, seq], TERMS_LOW, {"dp": p})
        for g in late:
            far_correlation(g)
        send_back(count, own - count)

        whole_wait(lag_in.at[0], s_recv.at[TERMS_LOW])
        summed = lag_in[0, 0]
        for b in range(1, seqs):
            summed = summed + lag_in[0, b]
        lag_fin[...] = summed * scale

        @pl.when(seq < seqs // 2)
        def _():
            whole_wait(lag_in.at[1], s_recv.at[TERMS_HIGH])
            more = lag_in[1, 0]
            for b in range(1, seqs):
                more = more + lag_in[1, b]
            lag_fin[...] += more * scale

        def deliver(k, carry):
            at = seq * part + k % part
            to = (seq + k // part) % seqs

            @pl.when((at != me) | (to != seq))
            def _():
                send(lag_fin.at[k % part], gf_all.at[h], FINAL, {"dp": to, "context": at})

            return carry

        lax.fori_loop(0, owners, deliver, 0)

        @pl.when(me // part == seq)
        def _():
            local(lag_fin.at[me % part], gf_all.at[h], FINAL)

        whole_wait(back_all, s_recv.at[BACK])

    gi_out[...] = (back_all[...].astype(F32) + direct[...]).astype(BF16)
    whole_wait(gf_all, s_recv.at[FINAL])
    for o in range(half):
        gf_out[own * o : own * (o + 1), :] = gf_all[o]

    others = own * (half - 1)
    for k in range(2):
        whole_wait(g_hbm.at[pl.ds(0, count * (half - 1))], s_send.at[NEAR_GRAD + k])
        whole_wait(x_hbm.at[pl.ds(0, count * (half - 1))], s_send.at[NEAR_IN + k])
    whole_wait(back_all.at[pl.ds(0, others)], s_send.at[BACK])

    @pl.when(is_high)
    def _():
        whole_wait(f_send, s_send.at[TAPS_HIGH])
        whole_wait(near_grad(0), s_send.at[FAR_GRAD])
        for g in range(count, own):
            whole_wait(far_grad(g, 1), s_send.at[FAR_GRAD + 1 + g - count])
        whole_wait(lag_send.at[pl.ds(0, part * (seqs // 2))], s_send.at[TERMS_HIGH])

    @pl.when(is_low)
    def _():
        whole_wait(f_all.at[pl.ds(0, half - 1)], s_send.at[TAPS_LOW])
        whole_wait(f_all.at[pl.ds(0, half)], s_send.at[TAPS_CROSS])
        whole_wait(lag_send.at[pl.ds(0, part * (seqs - 1))], s_send.at[TERMS_LOW])

        @pl.when(me // part == seq)
        def _():
            whole_wait(lag_send.at[pl.ds(0, owners - 1)], s_send.at[FINAL])

        @pl.when(me // part != seq)
        def _():
            whole_wait(lag_send, s_send.at[FINAL])


def stay(array):
    return pltpu.with_memory_space_constraint(array, pltpu.HBM)


def per_device(inputs, out_grad, filters, skip):
    channels, tok = inputs.shape[1], inputs.shape[2]
    groups = filters.shape[0]
    owners, seqs = lax.axis_size("context"), lax.axis_size("dp")
    half = owners // 2
    own = groups // half
    blocks = half // 2
    part = owners // seqs
    scale = 1.0 / math.sqrt(seqs * GROUP * tok * owners)
    vmem = pl.BlockSpec(memory_space=pltpu.VMEM)
    hbm = pl.BlockSpec(memory_space=pltpu.HBM)
    tiles = (groups, GROUP, LANES)
    held = (2, own, blocks, GROUP, LANES)
    grad_input, grad_filter = pl.pallas_call(
        functools.partial(kernel, (owners, seqs, scale)),
        out_shape=(
            jax.ShapeDtypeStruct(tiles, BF16),
            jax.ShapeDtypeStruct((groups, LANES), F32),
        ),
        in_specs=[hbm, hbm, hbm, hbm],
        out_specs=(vmem, vmem),
        scratch_shapes=[
            pltpu.VMEM((groups, LANES), F32),
            pltpu.VMEM((channels // LANES, LANES), F32),
            pltpu.VMEM(tiles, BF16),
            pltpu.VMEM((half, own, LANES), F32),
            pltpu.VMEM((owners, own, LANES), F32),
            pltpu.VMEM((2, own, 2 * blocks, GROUP, LANES), BF16),
            pltpu.VMEM((2, own, 3 * blocks, GROUP, LANES), BF16),
            pltpu.VMEM(held, BF16),
            pltpu.VMEM((own, PAIR, blocks * GROUP), BF16),
            pltpu.VMEM((own, LANES, LANES * (owners + 1)), BF16),
            pltpu.VMEM((own, blocks * GROUP, PAIR), F32),
            pltpu.VMEM(held, BF16),
            pltpu.VMEM(tiles, BF16),
            pltpu.VMEM(tiles, F32),
            pltpu.VMEM((own, LANES, LANES * owners), F32),
            pltpu.VMEM((owners, own, LANES), F32),
            pltpu.VMEM((2, seqs, part, own, LANES), F32),
            pltpu.VMEM((part, own, LANES), F32),
            pltpu.VMEM((half, own, LANES), F32),
            pltpu.SemaphoreType.DMA((N_SEMS,)),
            pltpu.SemaphoreType.DMA((N_SEMS,)),
            pltpu.SemaphoreType.DMA((3,)),
            pltpu.SemaphoreType.REGULAR,
        ],
        compiler_params=pltpu.CompilerParams(
            collective_id=0, has_side_effects=True, vmem_limit_bytes=28 * 1024 * 1024),
    )(
        stay(inputs.reshape(tiles)),
        stay(out_grad.reshape(tiles)),
        stay(filters),
        stay(skip.reshape(channels // LANES, LANES)),
    )
    return grad_input.reshape(1, channels, tok), grad_filter


def solution(mesh):
    placed = (
        P("dp", "tensor", "context"),
        P("dp", "tensor", "context"),
        P("tensor", "context"),
        P("tensor"),
    )
    return jax.shard_map(
        per_device,
        mesh=mesh,
        in_specs=placed,
        out_specs=(P("dp", "tensor", "context"), P("tensor", "context")),
        check_vma=False,
    )
```
